512 devices in a mesh: pair: 32 (over x, z_lo, core), col: 16 (over z_hi, y).
Axes of the slice: x: 4, y: 8, z: 8 (z_hi: 2, z_lo: 4; z = z_hi * 4 + z_lo), core: 2. Of those that a mesh axis runs over, the one named last changes fastest.
Arguments:
- two_rdm: bfloat16 [128, 128, 128, 128], P('pair', None, 'col'), may hold values from -6 to 6
- one_rdm: float32 [128, 128], replicated, may hold values from -6 to 6
- panel_block: int32 [1], replicated, may hold values from 0 to 15
Outputs:
- updated: bfloat16 [128, 128, 128, 128], P('pair', None, 'col')
- triangle: float32 [512, 512], replicated
The draws below stay inside these ranges and needn't reach their ends.
Inputs may be any that keep to these rules, and one draw needn't show every extreme that they name: The panel's first value of r is 4 * panel_block[0], below 64.
All inputs are finite; a program needn't handle non-finite values.
Results may differ from the reference program's by a relative error of at most 0.007.
Values may be sent and summed in bfloat16 or wider, within the bound.
A program may use at most 64 MiB of HBM per device.

```python
import jax
import jax.numpy as jnp
from jax import lax

ORB = 128
RPAN = 4
NB = 512


def block_levels(key, extent, cuts, smallest, largest):
    level, own = 1.0, jax.random.fold_in(key, 6)
    for position, shards_of in cuts:
        draws = jnp.exp(jax.random.uniform(jax.random.fold_in(own, position), (shards_of,), jnp.float32, smallest / len(cuts), largest / len(cuts)))
        level = level * jnp.repeat(draws, extent[position] // shards_of).reshape([-1 if axis == position else 1 for axis in range(len(extent))])
    return level


def centred(stream_key, shape, spread, most, cuts=(), kind=jnp.bfloat16):
    entries = spread * jax.random.normal(stream_key, shape, jnp.float32)
    if cuts:
        entries = entries * block_levels(stream_key, shape, cuts, -0.22, 0.18)
    return jnp.clip(entries, -most, most).astype(kind)


def setup_inputs(seed: int = 0) -> dict:
    keys = jax.random.split(jax.random.key(seed), 4)
    return {
        "two_rdm": centred(keys[0], (ORB, ORB, ORB, ORB), 1.0, 6.0, ((0, 32), (2, 16))),
        "one_rdm": centred(keys[1], (ORB, ORB), 1.0, 6.0, (), jnp.float32),
        "panel_block": jax.random.randint(keys[2], (1,), 0, ORB // (2 * RPAN)).astype(jnp.int32),
    }


def lower_solve(lower_factor, right_side):
    return lax.linalg.triangular_solve(lower_factor, right_side, left_side=True, lower=True)

def reference(two_rdm, one_rdm, panel_block):
    orbitals = ORB
    first_orb = panel_block[0] * RPAN
    index_range = jnp.arange(orbitals, dtype=jnp.int32)
    diagonal_mask = (index_range[:, None] == index_range[None, :]).astype(jnp.float32)
    g_tensor = diagonal_mask[:, None, None, :] * one_rdm[None, :, :, None] - jnp.transpose(two_rdm, (3, 1, 2, 0)).astype(jnp.float32)
    g_matrix = g_tensor.astype(jnp.bfloat16).reshape(orbitals * orbitals, orbitals * orbitals)
    panel = lax.dynamic_slice_in_dim(g_matrix, (first_orb * orbitals).astype(jnp.int32), NB, 1)
    gram = jnp.dot(panel.T.astype(jnp.float32), panel.astype(jnp.float32), preferred_element_type=jnp.float32)
    lower_factor = jnp.linalg.cholesky(gram)
    basis = lower_solve(lower_factor, panel.T.astype(jnp.float32)).T.astype(jnp.bfloat16)
    sums_t = jnp.dot(g_matrix.T.astype(jnp.float32), panel.astype(jnp.float32), preferred_element_type=jnp.float32)
    weights_t = lower_solve(lower_factor, sums_t.T).T.astype(jnp.bfloat16)
    updated = g_matrix.astype(jnp.float32) - jnp.dot(basis.astype(jnp.float32), weights_t.T.astype(jnp.float32), preferred_element_type=jnp.float32)
    col_orb = jnp.arange(orbitals * orbitals, dtype=jnp.int32) // orbitals
    trailing = col_orb >= first_orb + RPAN
    result = jnp.where(trailing[None, :], updated, g_matrix.astype(jnp.float32)).astype(jnp.bfloat16)
    return (result.reshape(orbitals, orbitals, orbitals, orbitals), lower_factor.T / orbitals)
```

```python
import functools

import jax
import jax.numpy as jnp
from jax import lax
from jax.experimental import pallas as pl
from jax.experimental.pallas import tpu as pltpu
from jax.sharding import PartitionSpec as P

RPAN = 4
BLOCK = 128
STRIP = 4
EXACT = lax.Precision.HIGHEST


def factor_block(work):
    for k in range(0, BLOCK, STRIP):
        r0 = (k // 8) * 8
        left = work[r0:BLOCK, 0:BLOCK]
        cols = [jnp.broadcast_to(left[:, k + j : k + j + 1], (BLOCK - r0, BLOCK)) for j in range(STRIP)]
        rows = [work[k + j : k + j + 1, :] for j in range(STRIP)]
        entry = {(i, j): cols[j][k + i - r0 : k + i - r0 + 1, :] for j in range(STRIP) for i in range(j, STRIP)}
        for j in range(STRIP):
            inv = lax.rsqrt(entry[j, j])
            rows[j] = rows[j] * jnp.concatenate([inv, inv], axis=1)
            cols[j] = cols[j] * inv
            low = {i: entry[i, j] * inv for i in range(j + 1, STRIP)}
            for i in range(j + 1, STRIP):
                for m in range(j + 1, i + 1):
                    entry[i, m] = entry[i, m] - low[i] * low[m]
                rows[i] = rows[i] - jnp.concatenate([low[i], low[i]], axis=1) * rows[j]
                cols[i] = cols[i] - low[i] * cols[j]
        for j in range(STRIP):
            work[k + j : k + j + 1, :] = rows[j]
        t0 = k + STRIP
        if t0 < BLOCK:
            s0 = (t0 // 8) * 8
            delta_a, delta_b = 0.0, 0.0
            for j in range(STRIP):
                c = cols[j][s0 - r0 :, :]
                delta_a = delta_a + c * rows[j][:, :BLOCK]
                delta_b = delta_b + c * rows[j][:, BLOCK:]
            if s0 < t0:
                below = lax.broadcasted_iota(jnp.int32, (BLOCK - s0, BLOCK), 0) + s0 >= t0
                delta_a = jnp.where(below, delta_a, 0.0)
                delta_b = jnp.where(below, delta_b, 0.0)
            work[s0:BLOCK, :BLOCK] = work[s0:BLOCK, :BLOCK] - delta_a
            work[s0:BLOCK, BLOCK:] = work[s0:BLOCK, BLOCK:] - delta_b


def factor_kernel(scale, gram_ref, tri_ref, inv_ref, aug, work):
    n = gram_ref.shape[0]
    row = lax.broadcasted_iota(jnp.int32, (n, n), 0)
    col = lax.broadcasted_iota(jnp.int32, (n, n), 1)
    aug[:, :n] = gram_ref[...]
    aug[:, n:] = (row == col).astype(jnp.float32)
    eye = (
        lax.broadcasted_iota(jnp.int32, (BLOCK, BLOCK), 0) == lax.broadcasted_iota(jnp.int32, (BLOCK, BLOCK), 1)
    ).astype(jnp.float32)

    def step(b, carry):
        o = pl.multiple_of(b * BLOCK, BLOCK)
        work[:, :BLOCK] = aug[pl.ds(o, BLOCK), pl.ds(o, BLOCK)]
        work[:, BLOCK:] = eye
        factor_block(work)
        aug[pl.ds(o, BLOCK), :] = jnp.dot(
            work[:, BLOCK:], aug[pl.ds(o, BLOCK), :], precision=EXACT, preferred_element_type=jnp.float32
        )

        def trail(m, carry):
            q = pl.multiple_of(m * BLOCK, BLOCK)
            u = aug[pl.ds(o, BLOCK), pl.ds(q, BLOCK)]
            aug[pl.ds(q, BLOCK), :] -= lax.dot_general(
                u, aug[pl.ds(o, BLOCK), :], (((0,), (0,)), ((), ())), precision=EXACT, preferred_element_type=jnp.float32
            )
            return carry

        return lax.fori_loop(b + 1, n // BLOCK, trail, carry)

    lax.fori_loop(0, n // BLOCK, step, 0)
    tri_ref[...] = jnp.where(row <= col, aug[:, :n], 0.0) / scale
    inv_ref[...] = jnp.where(row >= col, aug[:, n:], 0.0)


def factor(gram, scale):
    n = gram.shape[0]
    whole = pl.BlockSpec(memory_space=pltpu.VMEM)
    return pl.pallas_call(
        functools.partial(factor_kernel, scale),
        out_shape=(jax.ShapeDtypeStruct((n, n), jnp.float32),) * 2,
        in_specs=[whole],
        out_specs=(whole,) * 2,
        scratch_shapes=[pltpu.VMEM((n, 2 * n), jnp.float32), pltpu.VMEM((BLOCK, 2 * BLOCK), jnp.float32)],
        compiler_params=pltpu.CompilerParams(vmem_limit_bytes=16 << 20),
        cost_estimate=pl.CostEstimate(flops=4 * n**3, bytes_accessed=12 * n * n, transcendentals=n),
        name="panel_factor",
    )(gram)


def share(value, axis):
    count = lax.axis_size(axis)
    return lax.all_to_all(jnp.broadcast_to(value[None], (count, *value.shape)), axis, 0, 0)


def collect(value, axis):
    count = lax.axis_size(axis)
    return lax.all_to_all(value.reshape(count, value.shape[0] // count, *value.shape[1:]), axis, 0, 0)


def build_block(moved, s_index, one_cols):
    orbitals = moved.shape[0]
    diagonal_mask = (s_index[:, None] == jnp.arange(orbitals, dtype=jnp.int32)[None, :]).astype(jnp.float32)
    combined = diagonal_mask[:, None, None, :] * one_cols[None, :, :, None] - jnp.transpose(
        moved, (3, 1, 2, 0)
    ).astype(jnp.float32)
    return combined.astype(jnp.bfloat16)


def per_device(two_rdm, one_rdm, panel_block):
    q_count, orbitals, r_count, _ = two_rdm.shape
    groups = lax.axis_size("pair")
    s_count = orbitals // groups
    panel_width = RPAN * orbitals
    pair_index = lax.axis_index("pair")
    col_index = lax.axis_index("col")
    first_orb = panel_block[0] * RPAN
    s_index = pair_index * s_count + jnp.arange(s_count, dtype=jnp.int32)
    one_cols = lax.dynamic_slice_in_dim(one_rdm, col_index * r_count, r_count, 1)
    moved = lax.all_to_all(two_rdm, "pair", split_axis=3, concat_axis=0, tiled=True)
    row_count = s_count * orbitals
    col_count = r_count * orbitals
    local_tile = build_block(moved, s_index, one_cols).reshape(row_count, col_count)
    owner_col = first_orb // r_count
    within = first_orb % r_count
    panel_cols = lax.dynamic_slice_in_dim(local_tile, within * orbitals, panel_width, 1)
    mine = lax.dynamic_index_in_dim(collect(panel_cols, "col"), owner_col, 0, keepdims=False)
    panel = share(mine, "col").reshape(row_count, panel_width)
    gram_part = lax.dot_general(panel, panel, (((0,), (0,)), ((), ())), preferred_element_type=jnp.float32)
    gram = share(collect(gram_part, "pair").sum(0), "pair").reshape(panel_width, panel_width)
    triangle, inverse = factor(gram, orbitals)
    sums_part = lax.dot_general(
        local_tile, panel, (((0,), (0,)), ((), ())), preferred_element_type=jnp.float32
    ).astype(jnp.bfloat16)
    sums_mine = collect(sums_part, "pair").astype(jnp.float32).sum(0).astype(jnp.bfloat16)
    sums_t = share(sums_mine, "pair").reshape(col_count, panel_width)
    inverse_hi = inverse.astype(jnp.bfloat16)
    inverse_lo = (inverse - inverse_hi.astype(jnp.float32)).astype(jnp.bfloat16)

    def solve_right(value):
        dims = (((1,), (1,)), ((), ()))
        return (
            lax.dot_general(value, inverse_hi, dims, preferred_element_type=jnp.float32)
            + lax.dot_general(value, inverse_lo, dims, preferred_element_type=jnp.float32)
        ).astype(jnp.bfloat16)

    weights_t = solve_right(sums_t)
    basis = solve_right(panel)
    col_orb = col_index * r_count + jnp.arange(col_count, dtype=jnp.int32) // orbitals
    trailing = col_orb >= first_orb + RPAN
    product = lax.dot_general(basis, weights_t, (((1,), (1,)), ((), ())), preferred_element_type=jnp.float32)
    refreshed = local_tile.astype(jnp.float32) - product
    result = jnp.where(trailing[None, :], refreshed, local_tile.astype(jnp.float32)).astype(jnp.bfloat16)
    return (result.reshape(s_count, orbitals, r_count, orbitals), triangle)


def solution(mesh):
    return jax.shard_map(
        per_device,
        mesh=mesh,
        in_specs=(P("pair", None, "col", None), P(), P()),
        out_specs=(P("pair", None, "col", None), P()),
        check_vma=False,
    )
```

```python
import functools

import jax
import jax.numpy as jnp
from jax import lax
from jax.experimental import pallas as pl
from jax.experimental.pallas import tpu as pltpu
from jax.sharding import PartitionSpec as P

RPAN = 4
BLOCK = 128
STRIP = 4
EXACT = lax.Precision.HIGHEST
MESH = pl.DeviceIdType.MESH
Y = 8


def factor_block(work):
    for k in range(0, BLOCK, STRIP):
        r0 = (k // 8) * 8
        left = work[r0:BLOCK, 0:BLOCK]
        cols = [jnp.broadcast_to(left[:, k + j : k + j + 1], (BLOCK - r0, BLOCK)) for j in range(STRIP)]
        rows = [work[k + j : k + j + 1, :] for j in range(STRIP)]
        entry = {(i, j): cols[j][k + i - r0 : k + i - r0 + 1, :] for j in range(STRIP) for i in range(j, STRIP)}
        for j in range(STRIP):
            inv = lax.rsqrt(entry[j, j])
            rows[j] = rows[j] * jnp.concatenate([inv, inv], axis=1)
            cols[j] = cols[j] * inv
            low = {i: entry[i, j] * inv for i in range(j + 1, STRIP)}
            for i in range(j + 1, STRIP):
                for m in range(j + 1, i + 1):
                    entry[i, m] = entry[i, m] - low[i] * low[m]
                rows[i] = rows[i] - jnp.concatenate([low[i], low[i]], axis=1) * rows[j]
                cols[i] = cols[i] - low[i] * cols[j]
        for j in range(STRIP):
            work[k + j : k + j + 1, :] = rows[j]
        t0 = k + STRIP
        if t0 < BLOCK:
            s0 = (t0 // 8) * 8
            delta_a, delta_b = 0.0, 0.0
            for j in range(STRIP):
                c = cols[j][s0 - r0 :, :]
                delta_a = delta_a + c * rows[j][:, :BLOCK]
                delta_b = delta_b + c * rows[j][:, BLOCK:]
            if s0 < t0:
                below = lax.broadcasted_iota(jnp.int32, (BLOCK - s0, BLOCK), 0) + s0 >= t0
                delta_a = jnp.where(below, delta_a, 0.0)
                delta_b = jnp.where(below, delta_b, 0.0)
            work[s0:BLOCK, :BLOCK] = work[s0:BLOCK, :BLOCK] - delta_a
            work[s0:BLOCK, BLOCK:] = work[s0:BLOCK, BLOCK:] - delta_b


def factor_kernel(scale, gram_ref, tri_ref, inv_ref, aug, work):
    n = gram_ref.shape[0]
    row = lax.broadcasted_iota(jnp.int32, (n, n), 0)
    col = lax.broadcasted_iota(jnp.int32, (n, n), 1)
    aug[:, :n] = gram_ref[...]
    aug[:, n:] = (row == col).astype(jnp.float32)
    eye = (
        lax.broadcasted_iota(jnp.int32, (BLOCK, BLOCK), 0) == lax.broadcasted_iota(jnp.int32, (BLOCK, BLOCK), 1)
    ).astype(jnp.float32)

    def step(b, carry):
        o = pl.multiple_of(b * BLOCK, BLOCK)
        work[:, :BLOCK] = aug[pl.ds(o, BLOCK), pl.ds(o, BLOCK)]
        work[:, BLOCK:] = eye
        factor_block(work)
        aug[pl.ds(o, BLOCK), :] = jnp.dot(
            work[:, BLOCK:], aug[pl.ds(o, BLOCK), :], precision=EXACT, preferred_element_type=jnp.float32
        )

        def trail(m, carry):
            q = pl.multiple_of(m * BLOCK, BLOCK)
            u = aug[pl.ds(o, BLOCK), pl.ds(q, BLOCK)]
            aug[pl.ds(q, BLOCK), :] -= lax.dot_general(
                u, aug[pl.ds(o, BLOCK), :], (((0,), (0,)), ((), ())), precision=EXACT, preferred_element_type=jnp.float32
            )
            return carry

        return lax.fori_loop(b + 1, n // BLOCK, trail, carry)

    lax.fori_loop(0, n // BLOCK, step, 0)
    tri_ref[...] = jnp.where(row <= col, aug[:, :n], 0.0) / scale
    inv_ref[...] = jnp.where(row >= col, aug[:, n:], 0.0)


def factor(gram, scale):
    n = gram.shape[0]
    whole = pl.BlockSpec(memory_space=pltpu.VMEM)
    return pl.pallas_call(
        functools.partial(factor_kernel, scale),
        out_shape=(jax.ShapeDtypeStruct((n, n), jnp.float32),) * 2,
        in_specs=[whole],
        out_specs=(whole,) * 2,
        scratch_shapes=[pltpu.VMEM((n, 2 * n), jnp.float32), pltpu.VMEM((BLOCK, 2 * BLOCK), jnp.float32)],
        compiler_params=pltpu.CompilerParams(vmem_limit_bytes=16 << 20),
        cost_estimate=pl.CostEstimate(flops=4 * n**3, bytes_accessed=12 * n * n, transcendentals=n),
        name="panel_factor",
    )(gram)


def exchange_kernel(owner_ref, cand_ref, tile_ref, panel_ref, gram_ref, mine_ref,
                    picks, gpart, gin, spart, score, shalf, sin,
                    p_send, p_recv, q_send, q_recv, g1_send, g1_recv, g2_send, g2_recv,
                    g3_send, g3_recv, g4_send, g4_recv, s1_send, s1_recv, s2_send, s2_recv):
    pair = lax.axis_index("pair")
    colm = lax.axis_index("col")
    n_pair = lax.axis_size("pair")
    n_chip = n_pair // 2
    chip, core = pair // 2, lax.rem(pair, 2)
    half, y = colm // Y, lax.rem(colm, Y)
    other_core = 2 * chip + 1 - core
    part = cand_ref.shape[0] // Y
    width = cand_ref.shape[1]

    barrier = pltpu.get_barrier_semaphore()

    def greet_pair(d, carry):
        pl.semaphore_signal(barrier, inc=1, device_id={"pair": lax.rem(pair + d, n_pair)}, device_id_type=MESH)
        return carry

    def greet_y(d, carry):
        pl.semaphore_signal(barrier, inc=1, device_id={"col": half * Y + lax.rem(y + d, Y)}, device_id_type=MESH)
        return carry

    lax.fori_loop(1, n_pair, greet_pair, 0)
    lax.fori_loop(1, Y, greet_y, 0)
    pl.semaphore_signal(barrier, inc=1, device_id={"col": (1 - half) * Y + y}, device_id_type=MESH)
    pl.semaphore_wait(barrier, n_pair + Y - 1)

    def rows_of(ref, k):
        return ref.at[pl.ds(pl.multiple_of(k * part, part), part)]

    def offer(k):
        return pltpu.make_async_remote_copy(
            src_ref=rows_of(cand_ref, k), dst_ref=picks.at[y], send_sem=p_send.at[k], recv_sem=p_recv.at[y],
            device_id={"col": k}, device_id_type=MESH)

    def offered(k):
        return pltpu.make_async_remote_copy(
            src_ref=rows_of(cand_ref, k), dst_ref=picks.at[k], send_sem=p_send.at[k], recv_sem=p_recv.at[k],
            device_id={"col": k}, device_id_type=MESH)

    def across():
        return pltpu.make_async_remote_copy(
            src_ref=rows_of(panel_ref, y), dst_ref=rows_of(panel_ref, y), send_sem=q_send.at[0], recv_sem=q_recv.at[0],
            device_id={"col": (1 - half) * Y + y}, device_id_type=MESH)

    def gather(k):
        return pltpu.make_async_remote_copy(
            src_ref=rows_of(panel_ref, y), dst_ref=rows_of(panel_ref, y), send_sem=g2_send.at[0, k], recv_sem=g2_recv.at[0, y],
            device_id={"col": half * Y + k}, device_id_type=MESH)

    def gathered(k):
        return pltpu.make_async_remote_copy(
            src_ref=rows_of(panel_ref, y), dst_ref=rows_of(panel_ref, k), send_sem=g2_send.at[0, k], recv_sem=g2_recv.at[0, k],
            device_id={"col": half * Y + k}, device_id_type=MESH)

    @pl.when(half == 0)
    def _():
        lax.fori_loop(1, Y, lambda d, c: (offer(lax.rem(y + d, Y)).start(), c)[1], 0)
        picks[y] = cand_ref[pl.ds(pl.multiple_of(y * part, part), part), :]
        lax.fori_loop(1, Y, lambda d, c: (offered(lax.rem(y + d, Y)).wait_recv(), c)[1], 0)
        panel_ref[pl.ds(pl.multiple_of(y * part, part), part), :] = picks[owner_ref[0]]
        across().start()

    @pl.when(half == 1)
    def _():
        across().wait_recv()

    lax.fori_loop(1, Y, lambda d, c: (gather(lax.rem(y + d, Y)).start(), c)[1], 0)
    lax.fori_loop(1, Y, lambda d, c: (gathered(lax.rem(y + d, Y)).wait_recv(), c)[1], 0)

    over_rows = (((0,), (0,)), ((), ()))
    lead = pl.multiple_of((y // 2) * BLOCK, BLOCK)
    gpart[...] = lax.dot_general(panel_ref[:, pl.ds(lead, BLOCK)], panel_ref[...], over_rows,
                                 preferred_element_type=jnp.float32)
    base = lax.rem(y, 2) * part
    wide = width // BLOCK

    def piece(i):
        return gpart.at[pl.ds(pl.multiple_of(base + (i // wide) * 8, 8), 8),
                        pl.ds(pl.multiple_of(lax.rem(i, wide) * BLOCK, BLOCK), BLOCK)]

    def g1(i, slot):
        return pltpu.make_async_remote_copy(
            src_ref=piece(i), dst_ref=gin.at[slot], send_sem=g1_send.at[i], recv_sem=g1_recv.at[slot],
            device_id={"pair": i}, device_id_type=MESH)

    lax.fori_loop(1, n_pair, lambda d, c: (g1(lax.rem(pair + d, n_pair), pair).start(), c)[1], 0)
    gin[pair] = gpart[pl.ds(pl.multiple_of(base + (pair // wide) * 8, 8), 8),
                      pl.ds(pl.multiple_of(lax.rem(pair, wide) * BLOCK, BLOCK), BLOCK)]

    def products(k, c):
        lane = pl.multiple_of(k * 2 * BLOCK, 2 * BLOCK)
        out = lax.dot_general(tile_ref[:, pl.ds(lane, 2 * BLOCK)], panel_ref[...], over_rows,
                              preferred_element_type=jnp.float32).astype(jnp.bfloat16)
        count = 2 * BLOCK // (2 * chunk)
        spart[pl.ds(k * count, count)] = out.reshape(count, 2, chunk, width)
        return c

    chunk = tile_ref.shape[1] // n_pair
    lax.fori_loop(0, tile_ref.shape[1] // (2 * BLOCK), products, 0)

    def s1():
        return pltpu.make_async_remote_copy(
            src_ref=spart.at[:, 1 - core], dst_ref=score, send_sem=s1_send.at[0], recv_sem=s1_recv.at[0],
            device_id={"pair": other_core}, device_id_type=MESH)

    s1().start()

    lax.fori_loop(1, n_pair, lambda d, c: (g1(lax.rem(pair + d, n_pair), lax.rem(pair + d, n_pair)).wait_recv(), c)[1], 0)
    my_r, my_c = pair // wide, lax.rem(pair, wide)

    def column(ref_c):
        return pl.ds(pl.multiple_of(ref_c * BLOCK, BLOCK), BLOCK)

    gram_ref[y, my_r, :, column(my_c)] = jnp.sum(gin[...], axis=0)

    def g2(k, row):
        where = gram_ref.at[row, my_r, :, column(my_c)]
        return pltpu.make_async_remote_copy(
            src_ref=where, dst_ref=where, send_sem=g2_send.at[1, k], recv_sem=g2_recv.at[1, row],
            device_id={"col": half * Y + k}, device_id_type=MESH)

    lax.fori_loop(1, Y, lambda d, c: (g2(lax.rem(y + d, Y), y).start(), c)[1], 0)
    lax.fori_loop(1, Y, lambda d, c: (g2(lax.rem(y + d, Y), lax.rem(y + d, Y)).wait_recv(), c)[1], 0)

    def g3(t, source):
        where = gram_ref.at[:, source // wide, :, column(lax.rem(source, wide))]
        return pltpu.make_async_remote_copy(
            src_ref=where, dst_ref=where, send_sem=g3_send.at[t], recv_sem=g3_recv.at[source // 2],
            device_id={"pair": 2 * t + core}, device_id_type=MESH)

    def g4(source):
        where = gram_ref.at[:, source // wide, :, column(lax.rem(source, wide))]
        return pltpu.make_async_remote_copy(
            src_ref=where, dst_ref=where, send_sem=g4_send.at[source // 2], recv_sem=g4_recv.at[source // 2],
            device_id={"pair": other_core}, device_id_type=MESH)

    lax.fori_loop(1, n_chip, lambda d, c: (g3(lax.rem(chip + d, n_chip), pair).start(), c)[1], 0)
    g4(pair).start()

    s1().wait_recv()

    def add_cores(k, c):
        shalf[k] = (spart[k, core].astype(jnp.float32) + score[k].astype(jnp.float32)).astype(jnp.bfloat16)
        return c

    lax.fori_loop(0, n_chip, add_cores, 0)

    def s2(t, slot):
        return pltpu.make_async_remote_copy(
            src_ref=shalf.at[t], dst_ref=sin.at[slot], send_sem=s2_send.at[t], recv_sem=s2_recv.at[slot],
            device_id={"pair": 2 * t + core}, device_id_type=MESH)

    lax.fori_loop(1, n_chip, lambda d, c: (s2(lax.rem(chip + d, n_chip), chip).start(), c)[1], 0)
    sin[chip] = shalf[chip]

    def forward(d, c):
        t = lax.rem(chip + n_chip - d, n_chip)
        g3(t, 2 * t + core).wait_recv()
        g4(2 * t + core).start()
        return c

    lax.fori_loop(1, n_chip, forward, 0)
    lax.fori_loop(1, n_chip, lambda d, c: (s2(lax.rem(chip + d, n_chip), lax.rem(chip + d, n_chip)).wait_recv(), c)[1], 0)
    mine_ref[...] = jnp.sum(sin[...].astype(jnp.float32), axis=0).astype(jnp.bfloat16)
    lax.fori_loop(0, n_chip, lambda t, c: (g4(2 * t + 1 - core).wait_recv(), c)[1], 0)

    @pl.when(half == 0)
    def _():
        lax.fori_loop(1, Y, lambda d, c: (offer(lax.rem(y + d, Y)).wait_send(), c)[1], 0)
        across().wait_send()

    lax.fori_loop(1, Y, lambda d, c: (gather(lax.rem(y + d, Y)).wait_send(), c)[1], 0)
    lax.fori_loop(1, Y, lambda d, c: (g2(lax.rem(y + d, Y), y).wait_send(), c)[1], 0)
    lax.fori_loop(1, n_pair, lambda d, c: (g1(lax.rem(pair + d, n_pair), pair).wait_send(), c)[1], 0)
    s1().wait_send()
    lax.fori_loop(1, n_chip, lambda d, c: (g3(lax.rem(chip + d, n_chip), pair).wait_send(), c)[1], 0)
    lax.fori_loop(1, n_chip, lambda d, c: (s2(lax.rem(chip + d, n_chip), chip).wait_send(), c)[1], 0)
    lax.fori_loop(0, n_chip, lambda t, c: (g4(2 * t + core).wait_send(), c)[1], 0)


def exchange(owner, cand, tile):
    rows, width = cand.shape
    n_pair = lax.axis_size("pair")
    n_chip = n_pair // 2
    chunk = tile.shape[1] // n_pair
    vmem = pl.BlockSpec(memory_space=pltpu.VMEM)
    dma = pltpu.SemaphoreType.DMA
    f32, bf16 = jnp.float32, jnp.bfloat16
    sems = []
    for shape in ((Y,), (1,), (n_pair,), (2, Y), (n_chip,), (n_chip,), (1,), (n_chip,)):
        sems += [dma(shape), dma(shape)]
    return pl.pallas_call(
        exchange_kernel,
        out_shape=(
            jax.ShapeDtypeStruct((rows, width), bf16),
            jax.ShapeDtypeStruct((Y, width // Y // 8, 8, width), f32),
            jax.ShapeDtypeStruct((chunk, width), bf16),
        ),
        in_specs=[pl.BlockSpec(memory_space=pltpu.SMEM), vmem, vmem],
        out_specs=(vmem,) * 3,
        scratch_shapes=[
            pltpu.VMEM((Y, rows // Y, width), bf16),
            pltpu.VMEM((BLOCK, width), f32),
            pltpu.VMEM((n_pair, 8, BLOCK), f32),
            pltpu.VMEM((n_chip, 2, chunk, width), bf16),
            pltpu.VMEM((n_chip, chunk, width), bf16),
            pltpu.VMEM((n_chip, chunk, width), bf16),
            pltpu.VMEM((n_chip, chunk, width), bf16),
            *sems,
        ],
        compiler_params=pltpu.CompilerParams(collective_id=0, has_side_effects=True, vmem_limit_bytes=32 << 20),
        name="panel_exchange",
    )(owner, cand, tile)


def share(value, axis):
    count = lax.axis_size(axis)
    return lax.all_to_all(jnp.broadcast_to(value[None], (count, *value.shape)), axis, 0, 0)


def build_block(moved, s_index, one_cols):
    orbitals = moved.shape[0]
    diagonal_mask = (s_index[:, None] == jnp.arange(orbitals, dtype=jnp.int32)[None, :]).astype(jnp.float32)
    combined = diagonal_mask[:, None, None, :] * one_cols[None, :, :, None] - jnp.transpose(
        moved, (3, 1, 2, 0)
    ).astype(jnp.float32)
    return combined.astype(jnp.bfloat16)


def per_device(two_rdm, one_rdm, panel_block):
    q_count, orbitals, r_count, _ = two_rdm.shape
    groups = lax.axis_size("pair")
    s_count = orbitals // groups
    panel_width = RPAN * orbitals
    pair_index = lax.axis_index("pair")
    col_index = lax.axis_index("col")
    first_orb = panel_block[0] * RPAN
    s_index = pair_index * s_count + jnp.arange(s_count, dtype=jnp.int32)
    one_cols = lax.dynamic_slice_in_dim(one_rdm, col_index * r_count, r_count, 1)
    moved = lax.all_to_all(two_rdm, "pair", split_axis=3, concat_axis=0, tiled=True)
    row_count = s_count * orbitals
    col_count = r_count * orbitals
    local_tile = build_block(moved, s_index, one_cols).reshape(row_count, col_count)
    owner_col = first_orb // r_count
    within = first_orb % r_count
    panel_cols = lax.dynamic_slice_in_dim(local_tile, within * orbitals, panel_width, 1)
    panel, gram, sums_mine = exchange(owner_col[None], panel_cols, local_tile)
    triangle, inverse = factor(gram.reshape(panel_width, panel_width), orbitals)
    sums_t = share(sums_mine, "pair").reshape(col_count, panel_width)
    inverse_hi = inverse.astype(jnp.bfloat16)
    inverse_lo = (inverse - inverse_hi.astype(jnp.float32)).astype(jnp.bfloat16)

    def solve_right(value):
        dims = (((1,), (1,)), ((), ()))
        return (
            lax.dot_general(value, inverse_hi, dims, preferred_element_type=jnp.float32)
            + lax.dot_general(value, inverse_lo, dims, preferred_element_type=jnp.float32)
        ).astype(jnp.bfloat16)

    weights_t = solve_right(sums_t)
    basis = solve_right(panel)
    col_orb = col_index * r_count + jnp.arange(col_count, dtype=jnp.int32) // orbitals
    trailing = col_orb >= first_orb + RPAN
    product = lax.dot_general(basis, weights_t, (((1,), (1,)), ((), ())), preferred_element_type=jnp.float32)
    refreshed = local_tile.astype(jnp.float32) - product
    result = jnp.where(trailing[None, :], refreshed, local_tile.astype(jnp.float32)).astype(jnp.bfloat16)
    return (result.reshape(s_count, orbitals, r_count, orbitals), triangle)


def solution(mesh):
    return jax.shard_map(
        per_device,
        mesh=mesh,
        in_specs=(P("pair", None, "col", None), P(), P()),
        out_specs=(P("pair", None, "col", None), P()),
        check_vma=False,
    )
```

```python
import functools

import jax
import jax.numpy as jnp
from jax import lax
from jax.experimental import pallas as pl
from jax.experimental.pallas import tpu as pltpu
from jax.sharding import PartitionSpec as P

RPAN = 4
BLOCK = 128
STRIP = 4
EXACT = lax.Precision.HIGHEST
MESH = pl.DeviceIdType.MESH
PIECES = 2
Y = 8


def factor_block(work):
    for k in range(0, BLOCK, STRIP):
        r0 = (k // 8) * 8
        left = work[r0:BLOCK, 0:BLOCK]
        cols = [jnp.broadcast_to(left[:, k + j : k + j + 1], (BLOCK - r0, BLOCK)) for j in range(STRIP)]
        rows = [work[k + j : k + j + 1, :] for j in range(STRIP)]
        entry = {(i, j): cols[j][k + i - r0 : k + i - r0 + 1, :] for j in range(STRIP) for i in range(j, STRIP)}
        for j in range(STRIP):
            inv = lax.rsqrt(entry[j, j])
            rows[j] = rows[j] * jnp.concatenate([inv, inv], axis=1)
            cols[j] = cols[j] * inv
            low = {i: entry[i, j] * inv for i in range(j + 1, STRIP)}
            for i in range(j + 1, STRIP):
                for m in range(j + 1, i + 1):
                    entry[i, m] = entry[i, m] - low[i] * low[m]
                rows[i] = rows[i] - jnp.concatenate([low[i], low[i]], axis=1) * rows[j]
                cols[i] = cols[i] - low[i] * cols[j]
        for j in range(STRIP):
            work[k + j : k + j + 1, :] = rows[j]
        t0 = k + STRIP
        if t0 < BLOCK:
            s0 = (t0 // 8) * 8
            delta_a, delta_b = 0.0, 0.0
            for j in range(STRIP):
                c = cols[j][s0 - r0 :, :]
                delta_a = delta_a + c * rows[j][:, :BLOCK]
                delta_b = delta_b + c * rows[j][:, BLOCK:]
            if s0 < t0:
                below = lax.broadcasted_iota(jnp.int32, (BLOCK - s0, BLOCK), 0) + s0 >= t0
                delta_a = jnp.where(below, delta_a, 0.0)
                delta_b = jnp.where(below, delta_b, 0.0)
            work[s0:BLOCK, :BLOCK] = work[s0:BLOCK, :BLOCK] - delta_a
            work[s0:BLOCK, BLOCK:] = work[s0:BLOCK, BLOCK:] - delta_b


def factor_kernel(scale, gram_ref, tri_ref, inv_ref, aug, work):
    n = gram_ref.shape[0]
    row = lax.broadcasted_iota(jnp.int32, (n, n), 0)
    col = lax.broadcasted_iota(jnp.int32, (n, n), 1)
    aug[:, :n] = gram_ref[...]
    aug[:, n:] = (row == col).astype(jnp.float32)
    eye = (
        lax.broadcasted_iota(jnp.int32, (BLOCK, BLOCK), 0) == lax.broadcasted_iota(jnp.int32, (BLOCK, BLOCK), 1)
    ).astype(jnp.float32)

    def step(b, carry):
        o = pl.multiple_of(b * BLOCK, BLOCK)
        work[:, :BLOCK] = aug[pl.ds(o, BLOCK), pl.ds(o, BLOCK)]
        work[:, BLOCK:] = eye
        factor_block(work)
        aug[pl.ds(o, BLOCK), :] = jnp.dot(
            work[:, BLOCK:], aug[pl.ds(o, BLOCK), :], precision=EXACT, preferred_element_type=jnp.float32
        )

        def trail(m, carry):
            q = pl.multiple_of(m * BLOCK, BLOCK)
            u = aug[pl.ds(o, BLOCK), pl.ds(q, BLOCK)]
            aug[pl.ds(q, BLOCK), :] -= lax.dot_general(
                u, aug[pl.ds(o, BLOCK), :], (((0,), (0,)), ((), ())), precision=EXACT, preferred_element_type=jnp.float32
            )
            return carry

        return lax.fori_loop(b + 1, n // BLOCK, trail, carry)

    lax.fori_loop(0, n // BLOCK, step, 0)
    tri_ref[...] = jnp.where(row <= col, aug[:, :n], 0.0) / scale
    inv_ref[...] = jnp.where(row >= col, aug[:, n:], 0.0)


def factor(gram, scale):
    n = gram.shape[0]
    whole = pl.BlockSpec(memory_space=pltpu.VMEM)
    return pl.pallas_call(
        functools.partial(factor_kernel, scale),
        out_shape=(jax.ShapeDtypeStruct((n, n), jnp.float32),) * 2,
        in_specs=[whole],
        out_specs=(whole,) * 2,
        scratch_shapes=[pltpu.VMEM((n, 2 * n), jnp.float32), pltpu.VMEM((BLOCK, 2 * BLOCK), jnp.float32)],
        compiler_params=pltpu.CompilerParams(vmem_limit_bytes=16 << 20),
        cost_estimate=pl.CostEstimate(flops=4 * n**3, bytes_accessed=12 * n * n, transcendentals=n),
        name="panel_factor",
    )(gram)


def wrap(value, count):
    return jnp.where(value >= count, value - count, value)


def each(start, stop, body):
    lax.fori_loop(start, stop, lambda k, c: (body(k), c)[1], 0)


def exchange_kernel(owner_ref, x_ref, one_ref, panel_ref, gt_ref, gram_ref, mine_ref,
                    land, order, picks_a, picks_b, gpart, gin, spart, score, shalf, sin,
                    a_send, a_recv, p_send, p_recv, q_send, q_recv, c_send, c_recv, g1_send, g1_recv, g2_send, g2_recv,
                    g3_send, g3_recv, g4_send, g4_recv, s1_send, s1_recv, s2_send, s2_recv):
    pair = lax.axis_index("pair")
    colm = lax.axis_index("col")
    n_pair = lax.axis_size("pair")
    n_chip = n_pair // 2
    chip, core = pair // 2, lax.rem(pair, 2)
    half, y = colm // Y, lax.rem(colm, Y)
    other_core = 2 * chip + 1 - core
    width = panel_ref.shape[0]
    part = width // Y
    wide = width // BLOCK
    s_count = x_ref.shape[1]
    s_piece = s_count // PIECES
    over_last = (((1,), (1,)), ((), ()))
    picks = (picks_a, picks_b)

    def on_pair(src, dst, send, recv, k):
        return pltpu.make_async_remote_copy(
            src_ref=src, dst_ref=dst, send_sem=send, recv_sem=recv, device_id={"pair": k}, device_id_type=MESH)

    def on_col(src, dst, send, recv, k):
        return pltpu.make_async_remote_copy(
            src_ref=src, dst_ref=dst, send_sem=send, recv_sem=recv, device_id={"col": k}, device_id_type=MESH)

    barrier = pltpu.get_barrier_semaphore()
    each(1, n_pair, lambda d: pl.semaphore_signal(
        barrier, inc=1, device_id={"pair": wrap(pair + d, n_pair)}, device_id_type=MESH))
    each(1, Y, lambda d: pl.semaphore_signal(
        barrier, inc=1, device_id={"col": half * Y + wrap(y + d, Y)}, device_id_type=MESH))
    pl.semaphore_signal(barrier, inc=1, device_id={"col": (1 - half) * Y + y}, device_id_type=MESH)
    pl.semaphore_wait(barrier, n_pair + Y - 1)

    def first(k, peer, slot):
        ss = pl.ds(k * s_piece, s_piece)
        return on_pair(x_ref.at[peer, ss, 0], land.at[0, slot, ss], a_send.at[k, peer], a_recv.at[k, slot], peer)

    def second(peer, slot):
        return on_pair(x_ref.at[peer, :, 1], land.at[1, slot], a_send.at[PIECES, peer], a_recv.at[PIECES, slot], peer)

    for k in range(PIECES):
        each(1, n_pair, lambda d: first(k, wrap(pair + d, n_pair), pair).start())
    for h in range(2):
        land[h, pair] = x_ref[pair, :, h]

    row = lax.broadcasted_iota(jnp.int32, (width, width), 0)
    col = lax.broadcasted_iota(jnp.int32, (width, width), 1)
    q, r = row & (BLOCK - 1), row // BLOCK
    order[...] = (col == (q // 4) * 16 + r * 4 + (q & 3)).astype(jnp.float32).astype(jnp.bfloat16)
    q_row = lax.broadcasted_iota(jnp.int32, (BLOCK, BLOCK), 0)

    def build(h, s):
        moved = land[h, :, s].reshape(width, BLOCK)
        placed = jnp.dot(order[...], moved, preferred_element_type=jnp.float32)
        for r in range(wide):
            diagonal = jnp.where(q_row == pair * s_count + s, one_ref[pl.ds(h * wide + r, 1), :], 0.0)
            gt_ref[h, r * BLOCK:(r + 1) * BLOCK, s * BLOCK:(s + 1) * BLOCK] = (
                diagonal - placed[r * BLOCK:(r + 1) * BLOCK]).astype(jnp.bfloat16)

    span = s_piece * BLOCK

    def block(k, piece):
        return pl.ds(pl.multiple_of(k * part, part), part), pl.ds(piece * span, span)

    def offer(piece, k, slot):
        rows, lanes = block(k, piece)
        return on_col(gt_ref.at[0, rows, lanes], picks[piece].at[slot], p_send.at[piece, k], p_recv.at[piece, slot], k)

    def across(piece):
        where = panel_ref.at[block(y, piece)]
        return on_col(where, where, q_send.at[piece], q_recv.at[piece], (1 - half) * Y + y)

    def gather(piece, k, row):
        where = panel_ref.at[block(row, piece)]
        return on_col(where, where, c_send.at[piece, k], c_recv.at[piece, row], half * Y + k)

    for piece in range(PIECES):
        each(1, n_pair, lambda d: first(piece, wrap(pair + d, n_pair), wrap(pair + d, n_pair)).wait_recv())
        for s in range(piece * s_piece, (piece + 1) * s_piece):
            build(0, s)

        @pl.when(half == 0)
        def _():
            each(1, Y, lambda d: offer(piece, wrap(y + d, Y), y).start())
            rows, lanes = block(y, piece)
            picks[piece][y] = gt_ref[0, rows, lanes]

    each(1, n_pair, lambda d: second(wrap(pair + d, n_pair), pair).start())

    for piece in range(PIECES):
        @pl.when(half == 0)
        def _():
            each(1, Y, lambda d: offer(piece, wrap(y + d, Y), wrap(y + d, Y)).wait_recv())
            rows, lanes = block(y, piece)
            panel_ref[rows, lanes] = picks[piece][owner_ref[0]]
            across(piece).start()

        @pl.when(half == 1)
        def _():
            across(piece).wait_recv()

        each(1, Y, lambda d: gather(piece, wrap(y + d, Y), y).start())

    each(1, n_pair, lambda d: second(wrap(pair + d, n_pair), wrap(pair + d, n_pair)).wait_recv())
    for s in range(s_count):
        build(1, s)
    for piece in range(PIECES):
        each(1, Y, lambda d: gather(piece, wrap(y + d, Y), wrap(y + d, Y)).wait_recv())

    chunk = mine_ref.shape[0]
    rows_at_once = 2 * BLOCK
    count = rows_at_once // (2 * chunk)
    for h in range(2):
        for k in range(width // rows_at_once):
            out = lax.dot_general(gt_ref[h, k * rows_at_once:(k + 1) * rows_at_once, :], panel_ref[...], over_last,
                                  preferred_element_type=jnp.float32).astype(jnp.bfloat16)
            at = (h * (width // rows_at_once) + k) * count
            spart[at:at + count] = out.reshape(count, 2, chunk, width)

    def s1():
        return on_pair(spart.at[:, 1 - core], score, s1_send.at[0], s1_recv.at[0], other_core)

    s1().start()

    gpart[...] = lax.dot_general(panel_ref[pl.ds(pl.multiple_of(y * part, part), part), :], panel_ref[...], over_last,
                                 preferred_element_type=jnp.float32)

    def column(c):
        return pl.ds(pl.multiple_of(c * BLOCK, BLOCK), BLOCK)

    def g1(i, slot):
        src = gpart.at[pl.ds(pl.multiple_of((i // wide) * 8, 8), 8), column(lax.rem(i, wide))]
        return on_pair(src, gin.at[slot], g1_send.at[i], g1_recv.at[slot], i)

    each(1, n_pair, lambda d: g1(wrap(pair + d, n_pair), pair).start())
    my_r, my_c = pair // wide, lax.rem(pair, wide)
    gin[pair] = gpart[pl.ds(pl.multiple_of(my_r * 8, 8), 8), column(my_c)]

    s1().wait_recv()

    def add_cores(k):
        shalf[k] = (spart[k, core].astype(jnp.float32) + score[k].astype(jnp.float32)).astype(jnp.bfloat16)

    each(0, n_chip, add_cores)

    def s2(t, slot):
        return on_pair(shalf.at[t], sin.at[slot], s2_send.at[t], s2_recv.at[slot], 2 * t + core)

    each(1, n_chip, lambda d: s2(wrap(chip + d, n_chip), chip).start())
    sin[chip] = shalf[chip]

    each(1, n_pair, lambda d: g1(wrap(pair + d, n_pair), wrap(pair + d, n_pair)).wait_recv())
    gram_ref[y, my_r, :, column(my_c)] = jnp.sum(gin[...], axis=0)

    def g2(k, row):
        where = gram_ref.at[row, my_r, :, column(my_c)]
        return on_col(where, where, g2_send.at[k], g2_recv.at[row], half * Y + k)

    each(1, Y, lambda d: g2(wrap(y + d, Y), y).start())
    each(1, Y, lambda d: g2(wrap(y + d, Y), wrap(y + d, Y)).wait_recv())

    def held(source):
        return gram_ref.at[:, source // wide, :, column(lax.rem(source, wide))]

    def g3(t, source):
        return on_pair(held(source), held(source), g3_send.at[t], g3_recv.at[source // 2], 2 * t + core)

    def g4(source):
        return on_pair(held(source), held(source), g4_send.at[source // 2], g4_recv.at[source // 2], other_core)

    each(1, n_chip, lambda d: g3(wrap(chip + d, n_chip), pair).start())
    g4(pair).start()

    each(1, n_chip, lambda d: s2(wrap(chip + d, n_chip), wrap(chip + d, n_chip)).wait_recv())
    mine_ref[...] = jnp.sum(sin[...].astype(jnp.float32), axis=0).astype(jnp.bfloat16)

    def forward(d):
        source = 2 * wrap(chip + n_chip - d, n_chip) + core
        g3(source // 2, source).wait_recv()
        g4(source).start()

    each(1, n_chip, forward)
    each(0, n_chip, lambda t: g4(2 * t + 1 - core).wait_recv())

    for k in range(PIECES):
        each(1, n_pair, lambda d: first(k, wrap(pair + d, n_pair), pair).wait_send())
        each(1, Y, lambda d: gather(k, wrap(y + d, Y), y).wait_send())

        @pl.when(half == 0)
        def _():
            each(1, Y, lambda d: offer(k, wrap(y + d, Y), y).wait_send())
            across(k).wait_send()

    each(1, n_pair, lambda d: second(wrap(pair + d, n_pair), pair).wait_send())
    each(1, n_pair, lambda d: g1(wrap(pair + d, n_pair), pair).wait_send())
    each(1, Y, lambda d: g2(wrap(y + d, Y), y).wait_send())
    s1().wait_send()
    each(1, n_chip, lambda d: s2(wrap(chip + d, n_chip), chip).wait_send())
    each(1, n_chip, lambda d: g3(wrap(chip + d, n_chip), pair).wait_send())
    each(0, n_chip, lambda t: g4(2 * t + core).wait_send())


def exchange(owner, blocks, one_t):
    n_pair, s_count, _, packed, orbitals = blocks.shape
    n_chip = n_pair // 2
    width = n_pair * packed
    rows = s_count * orbitals
    chunk = 2 * width // n_pair
    vmem = pl.BlockSpec(memory_space=pltpu.VMEM)
    f32, bf16 = jnp.float32, jnp.bfloat16
    sems = []
    for shape in ((PIECES + 1, n_pair), (PIECES, Y), (PIECES,), (PIECES, Y), (n_pair,), (Y,), (n_chip,), (n_chip,),
                  (1,), (n_chip,)):
        sems += [pltpu.SemaphoreType.DMA(shape)] * 2
    return pl.pallas_call(
        exchange_kernel,
        out_shape=(
            jax.ShapeDtypeStruct((width, rows), bf16),
            jax.ShapeDtypeStruct((2, width, rows), bf16),
            jax.ShapeDtypeStruct((Y, width // Y // 8, 8, width), f32),
            jax.ShapeDtypeStruct((chunk, width), bf16),
        ),
        in_specs=[pl.BlockSpec(memory_space=pltpu.SMEM), vmem, vmem],
        out_specs=(vmem,) * 4,
        scratch_shapes=[
            pltpu.VMEM((2, n_pair, s_count, packed, orbitals), bf16),
            pltpu.VMEM((width, width), bf16),
            *[pltpu.VMEM((Y, width // Y, rows // PIECES), bf16)] * PIECES,
            pltpu.VMEM((width // Y, width), f32),
            pltpu.VMEM((n_pair, 8, BLOCK), f32),
            pltpu.VMEM((n_chip, 2, chunk, width), bf16),
            pltpu.VMEM((n_chip, chunk, width), bf16),
            pltpu.VMEM((n_chip, chunk, width), bf16),
            pltpu.VMEM((n_chip, chunk, width), bf16),
            *sems,
        ],
        compiler_params=pltpu.CompilerParams(collective_id=0, has_side_effects=True, vmem_limit_bytes=32 << 20),
        name="regroup_exchange",
    )(owner, blocks, one_t)


def share(value, axis):
    count = lax.axis_size(axis)
    return lax.all_to_all(jnp.broadcast_to(value[None], (count, *value.shape)), axis, 0, 0)


def per_device(two_rdm, one_rdm, panel_block):
    q_count, orbitals, r_count, _ = two_rdm.shape
    groups = lax.axis_size("pair")
    s_count = orbitals // groups
    panel_width = RPAN * orbitals
    col_index = lax.axis_index("col")
    first_orb = panel_block[0] * RPAN
    owner_col = first_orb // r_count
    within = first_orb % r_count
    turned = lax.dynamic_slice_in_dim(jnp.concatenate([two_rdm, two_rdm], 2), within, r_count, 2)
    blocks = jnp.transpose(turned, (3, 2, 0, 1)).reshape(groups, s_count, 2, RPAN * q_count, orbitals)
    one_cols = lax.dynamic_slice_in_dim(one_rdm, col_index * r_count, r_count, 1)
    one_t = lax.dynamic_slice_in_dim(jnp.concatenate([one_cols, one_cols], 1), within, r_count, 1).T
    panel_t, tile_t, gram, sums_mine = exchange(owner_col[None], blocks, one_t)
    triangle, inverse = factor(gram.reshape(panel_width, panel_width), orbitals)
    col_count = r_count * orbitals
    row_count = s_count * orbitals
    sums_t = share(sums_mine, "pair").reshape(col_count, panel_width)
    tile_t = tile_t.reshape(col_count, row_count)
    inverse_hi = inverse.astype(jnp.bfloat16)
    inverse_lo = (inverse - inverse_hi.astype(jnp.float32)).astype(jnp.bfloat16)

    def times(a, b, dims):
        return lax.dot_general(a, b, (dims, ((), ())), preferred_element_type=jnp.float32)

    weights_t = (times(sums_t, inverse_hi, ((1,), (1,))) + times(sums_t, inverse_lo, ((1,), (1,)))).astype(jnp.bfloat16)
    basis_t = (times(inverse_hi, panel_t, ((1,), (0,))) + times(inverse_lo, panel_t, ((1,), (0,)))).astype(jnp.bfloat16)
    col_orb = col_index * r_count + (jnp.arange(r_count, dtype=jnp.int32) + within) % r_count
    trailing = jnp.repeat(col_orb >= first_orb + RPAN, orbitals)
    product = times(weights_t, basis_t, ((1,), (0,)))
    kept = tile_t.astype(jnp.float32)
    result = jnp.where(trailing[:, None], kept - product, kept).astype(jnp.bfloat16)
    result = result.reshape(r_count, orbitals, s_count, orbitals)
    result = lax.dynamic_slice_in_dim(jnp.concatenate([result, result], 0), r_count - within, r_count, 0)
    return (jnp.transpose(result, (2, 3, 0, 1)), triangle)


def solution(mesh):
    return jax.shard_map(
        per_device,
        mesh=mesh,
        in_specs=(P("pair", None, "col", None), P(), P()),
        out_specs=(P("pair", None, "col", None), P()),
        check_vma=False,
    )
```

```python
import functools

import jax
import jax.numpy as jnp
from jax import lax
from jax.experimental import pallas as pl
from jax.experimental.pallas import tpu as pltpu
from jax.sharding import PartitionSpec as P

RPAN = 4
BLOCK = 128
STRIP = 4
EXACT = lax.Precision.HIGHEST
MESH = pl.DeviceIdType.MESH
PIECES = 2
Y = 8


def factor_block(work):
    for k in range(0, BLOCK, STRIP):
        r0 = (k // 8) * 8
        left = work[r0:BLOCK, 0:BLOCK]
        cols = [jnp.broadcast_to(left[:, k + j : k + j + 1], (BLOCK - r0, BLOCK)) for j in range(STRIP)]
        rows = [work[k + j : k + j + 1, :] for j in range(STRIP)]
        entry = {(i, j): cols[j][k + i - r0 : k + i - r0 + 1, :] for j in range(STRIP) for i in range(j, STRIP)}
        for j in range(STRIP):
            inv = lax.rsqrt(entry[j, j])
            rows[j] = rows[j] * jnp.concatenate([inv, inv], axis=1)
            cols[j] = cols[j] * inv
            low = {i: entry[i, j] * inv for i in range(j + 1, STRIP)}
            for i in range(j + 1, STRIP):
                for m in range(j + 1, i + 1):
                    entry[i, m] = entry[i, m] - low[i] * low[m]
                rows[i] = rows[i] - jnp.concatenate([low[i], low[i]], axis=1) * rows[j]
                cols[i] = cols[i] - low[i] * cols[j]
        for j in range(STRIP):
            work[k + j : k + j + 1, :] = rows[j]
        t0 = k + STRIP
        if t0 < BLOCK:
            s0 = (t0 // 8) * 8
            delta_a, delta_b = 0.0, 0.0
            for j in range(STRIP):
                c = cols[j][s0 - r0 :, :]
                delta_a = delta_a + c * rows[j][:, :BLOCK]
                delta_b = delta_b + c * rows[j][:, BLOCK:]
            if s0 < t0:
                below = lax.broadcasted_iota(jnp.int32, (BLOCK - s0, BLOCK), 0) + s0 >= t0
                delta_a = jnp.where(below, delta_a, 0.0)
                delta_b = jnp.where(below, delta_b, 0.0)
            work[s0:BLOCK, :BLOCK] = work[s0:BLOCK, :BLOCK] - delta_a
            work[s0:BLOCK, BLOCK:] = work[s0:BLOCK, BLOCK:] - delta_b


def finish_kernel(scale, flag_ref, gram_ref, sums_ref, panel_ref, tile_ref, tri_ref, out_ref, aug, work, outer):
    n = gram_ref.shape[0]
    row = lax.broadcasted_iota(jnp.int32, (n, n), 0)
    col = lax.broadcasted_iota(jnp.int32, (n, n), 1)
    aug[:, :n] = gram_ref[...]
    aug[:, n:] = (row == col).astype(jnp.float32)
    eye = (
        lax.broadcasted_iota(jnp.int32, (BLOCK, BLOCK), 0) == lax.broadcasted_iota(jnp.int32, (BLOCK, BLOCK), 1)
    ).astype(jnp.float32)

    def step(b, carry):
        o = pl.multiple_of(b * BLOCK, BLOCK)
        work[:, :BLOCK] = aug[pl.ds(o, BLOCK), pl.ds(o, BLOCK)]
        work[:, BLOCK:] = eye
        factor_block(work)
        aug[pl.ds(o, BLOCK), :] = jnp.dot(
            work[:, BLOCK:], aug[pl.ds(o, BLOCK), :], precision=EXACT, preferred_element_type=jnp.float32
        )

        def trail(m, carry):
            q = pl.multiple_of(m * BLOCK, BLOCK)
            u = aug[pl.ds(o, BLOCK), pl.ds(q, BLOCK)]
            aug[pl.ds(q, BLOCK), :] -= lax.dot_general(
                u, aug[pl.ds(o, BLOCK), :], (((0,), (0,)), ((), ())), precision=EXACT, preferred_element_type=jnp.float32
            )
            return carry

        return lax.fori_loop(b + 1, n // BLOCK, trail, carry)

    lax.fori_loop(0, n // BLOCK, step, 0)
    tri_ref[...] = jnp.where(row <= col, aug[:, :n], 0.0) / scale
    inverse = jnp.where(row >= col, aug[:, n:], 0.0)
    high = inverse.astype(jnp.bfloat16)
    low = (inverse - high.astype(jnp.float32)).astype(jnp.bfloat16)

    def times(a, b, dims):
        return lax.dot_general(a, b, (dims, ((), ())), preferred_element_type=jnp.float32)

    basis_t = (times(high, panel_ref[...], ((1,), (0,))) + times(low, panel_ref[...], ((1,), (0,)))).astype(jnp.bfloat16)
    s_count, orbitals, r_count, _ = out_ref.shape
    per_half = r_count // 2
    for h in range(2):
        source = flag_ref[2 + h]
        sums = sums_ref[source]
        weights_t = (times(sums, high, ((1,), (1,))) + times(sums, low, ((1,), (1,)))).astype(jnp.bfloat16)
        product = times(weights_t, basis_t, ((1,), (0,)))
        outer[h] = tile_ref[source].astype(jnp.float32) - jnp.where(flag_ref[h] > 0, product, 0.0)
    for s in range(s_count):
        parts = [
            outer[h, r * BLOCK:(r + 1) * BLOCK, s * orbitals:(s + 1) * orbitals].T
            for h in range(2) for r in range(per_half)
        ]
        out_ref[s] = jnp.stack(parts, axis=1).astype(jnp.bfloat16)


def finish(flags, gram, sums, panel_t, tile_t, s_count, scale):
    n = gram.shape[0]
    rows = panel_t.shape[1]
    whole = pl.BlockSpec(memory_space=pltpu.VMEM)
    return pl.pallas_call(
        functools.partial(finish_kernel, scale),
        out_shape=(
            jax.ShapeDtypeStruct((n, n), jnp.float32),
            jax.ShapeDtypeStruct((s_count, rows // s_count, 2 * n // BLOCK, BLOCK), jnp.bfloat16),
        ),
        in_specs=[pl.BlockSpec(memory_space=pltpu.SMEM)] + [whole] * 4,
        out_specs=(whole,) * 2,
        scratch_shapes=[
            pltpu.VMEM((n, 2 * n), jnp.float32),
            pltpu.VMEM((BLOCK, 2 * BLOCK), jnp.float32),
            pltpu.VMEM((2, n, rows), jnp.float32),
        ],
        compiler_params=pltpu.CompilerParams(vmem_limit_bytes=32 << 20),
        cost_estimate=pl.CostEstimate(flops=16 * n**3, bytes_accessed=24 * n * n, transcendentals=n),
        name="factor_apply",
    )(flags, gram, sums, panel_t, tile_t)


def wrap(value, count):
    return jnp.where(value >= count, value - count, value)


def each(start, stop, body):
    lax.fori_loop(start, stop, lambda k, c: (body(k), c)[1], 0)


def exchange_kernel(owner_ref, x_ref, one_ref, panel_ref, gt_ref, gram_ref, sums_ref,
                    land, order, picks_a, picks_b, gpart, gin, spart, score, shalf, sin,
                    a_send, a_recv, p_send, p_recv, q_send, q_recv, c_send, c_recv, g1_send, g1_recv, g2_send, g2_recv,
                    g3_send, g3_recv, h2_send, h2_recv, h3_send, h3_recv, g4_send, g4_recv,
                    s1_send, s1_recv, s2_send, s2_recv, s3_send, s3_recv, s4_send, s4_recv):
    pair = lax.axis_index("pair")
    colm = lax.axis_index("col")
    n_pair = lax.axis_size("pair")
    n_chip = n_pair // 2
    chip, core = pair // 2, lax.rem(pair, 2)
    half, y = colm // Y, lax.rem(colm, Y)
    other_core = 2 * chip + 1 - core
    width = panel_ref.shape[0]
    part = width // Y
    wide = width // BLOCK
    s_count = x_ref.shape[1]
    s_piece = s_count // PIECES
    over_last = (((1,), (1,)), ((), ()))
    picks = (picks_a, picks_b)

    def on_pair(src, dst, send, recv, k):
        return pltpu.make_async_remote_copy(
            src_ref=src, dst_ref=dst, send_sem=send, recv_sem=recv, device_id={"pair": k}, device_id_type=MESH)

    def on_col(src, dst, send, recv, k):
        return pltpu.make_async_remote_copy(
            src_ref=src, dst_ref=dst, send_sem=send, recv_sem=recv, device_id={"col": k}, device_id_type=MESH)

    barrier = pltpu.get_barrier_semaphore()
    each(1, n_pair, lambda d: pl.semaphore_signal(
        barrier, inc=1, device_id={"pair": wrap(pair + d, n_pair)}, device_id_type=MESH))
    each(1, Y, lambda d: pl.semaphore_signal(
        barrier, inc=1, device_id={"col": half * Y + wrap(y + d, Y)}, device_id_type=MESH))
    pl.semaphore_signal(barrier, inc=1, device_id={"col": (1 - half) * Y + y}, device_id_type=MESH)
    pl.semaphore_wait(barrier, n_pair + Y - 1)

    def first(k, peer, slot):
        ss = pl.ds(k * s_piece, s_piece)
        return on_pair(x_ref.at[peer, ss, 0], land.at[0, slot, ss], a_send.at[k], a_recv.at[k], peer)

    def second(peer, slot):
        return on_pair(x_ref.at[peer, :, 1], land.at[1, slot], a_send.at[PIECES], a_recv.at[PIECES], peer)

    def all_first(k):
        ss = pl.ds(k * s_piece, s_piece)
        return on_pair(x_ref.at[1:, ss, 0], land.at[0, 1:, ss], a_send.at[k], a_recv.at[k], other_core)

    def all_second():
        return on_pair(x_ref.at[1:, :, 1], land.at[1, 1:], a_send.at[PIECES], a_recv.at[PIECES], other_core)

    for k in range(PIECES):
        each(1, n_pair, lambda d: first(k, wrap(pair + d, n_pair), pair).start())
    for h in range(2):
        land[h, pair] = x_ref[pair, :, h]

    row = lax.broadcasted_iota(jnp.int32, (width, width), 0)
    col = lax.broadcasted_iota(jnp.int32, (width, width), 1)
    q, r = row & (BLOCK - 1), row // BLOCK
    order[...] = (col == (q // 4) * 16 + r * 4 + (q & 3)).astype(jnp.float32).astype(jnp.bfloat16)
    q_row = lax.broadcasted_iota(jnp.int32, (BLOCK, BLOCK), 0)

    def build(h, s):
        moved = land[h, :, s].reshape(width, BLOCK)
        placed = jnp.dot(order[...], moved, preferred_element_type=jnp.float32)
        for r in range(wide):
            diagonal = jnp.where(q_row == pair * s_count + s, one_ref[pl.ds(h * wide + r, 1), :], 0.0)
            gt_ref[h, r * BLOCK:(r + 1) * BLOCK, s * BLOCK:(s + 1) * BLOCK] = (
                diagonal - placed[r * BLOCK:(r + 1) * BLOCK]).astype(jnp.bfloat16)

    span = s_piece * BLOCK

    def block(k, piece):
        return pl.ds(pl.multiple_of(k * part, part), part), pl.ds(piece * span, span)

    def offer(piece, k, slot):
        rows, lanes = block(k, piece)
        return on_col(gt_ref.at[0, rows, lanes], picks[piece].at[slot], p_send.at[piece], p_recv.at[piece], k)

    def across(piece):
        where = panel_ref.at[block(y, piece)]
        return on_col(where, where, q_send.at[piece], q_recv.at[piece], (1 - half) * Y + y)

    def gather(piece, k, row):
        where = panel_ref.at[block(row, piece)]
        return on_col(where, where, c_send.at[piece], c_recv.at[piece], half * Y + k)

    def all_offers(piece):
        lanes = pl.ds(piece * span, span)
        return on_col(gt_ref.at[0, :(Y - 1) * part, lanes], picks[piece].at[1:], p_send.at[piece], p_recv.at[piece],
                      (1 - half) * Y + y)

    def all_gathers(piece):
        where = panel_ref.at[:(Y - 1) * part, pl.ds(piece * span, span)]
        return on_col(where, where, c_send.at[piece], c_recv.at[piece], (1 - half) * Y + y)

    for piece in range(PIECES):
        all_first(piece).wait_recv()
        for s in range(piece * s_piece, (piece + 1) * s_piece):
            build(0, s)

        @pl.when(half == 0)
        def _():
            each(1, Y, lambda d: offer(piece, wrap(y + d, Y), y).start())
            rows, lanes = block(y, piece)
            picks[piece][y] = gt_ref[0, rows, lanes]

    each(1, n_pair, lambda d: second(wrap(pair + d, n_pair), pair).start())

    for piece in range(PIECES):
        @pl.when(half == 0)
        def _():
            all_offers(piece).wait_recv()
            rows, lanes = block(y, piece)
            panel_ref[rows, lanes] = picks[piece][owner_ref[0]]
            across(piece).start()

        @pl.when(half == 1)
        def _():
            across(piece).wait_recv()

        each(1, Y, lambda d: gather(piece, wrap(y + d, Y), y).start())

    all_second().wait_recv()
    for s in range(s_count):
        build(1, s)
    for piece in range(PIECES):
        all_gathers(piece).wait_recv()

    chunk = sums_ref.shape[2]
    rows_at_once = 2 * BLOCK
    count = rows_at_once // (2 * chunk)
    for h in range(2):
        for k in range(width // rows_at_once):
            out = lax.dot_general(gt_ref[h, k * rows_at_once:(k + 1) * rows_at_once, :], panel_ref[...], over_last,
                                  preferred_element_type=jnp.float32).astype(jnp.bfloat16)
            at = (h * (width // rows_at_once) + k) * count
            spart[at:at + count] = out.reshape(count, 2, chunk, width)

    def s1():
        return on_pair(spart.at[:, 1 - core], score, s1_send.at[0], s1_recv.at[0], other_core)

    s1().start()

    gpart[...] = lax.dot_general(panel_ref[pl.ds(pl.multiple_of(y * part, part), part), :], panel_ref[...], over_last,
                                 preferred_element_type=jnp.float32)

    def column(c):
        return pl.ds(pl.multiple_of(c * BLOCK, BLOCK), BLOCK)

    def g1(i, slot):
        src = gpart.at[pl.ds(pl.multiple_of((i // wide) * 8, 8), 8), column(lax.rem(i, wide))]
        return on_pair(src, gin.at[slot], g1_send.at[0], g1_recv.at[0], i)

    each(1, n_pair, lambda d: g1(wrap(pair + d, n_pair), pair).start())
    my_r, my_c = pair // wide, lax.rem(pair, wide)
    gin[pair] = gpart[pl.ds(pl.multiple_of(my_r * 8, 8), 8), column(my_c)]

    s1().wait_recv()

    def add_cores(k):
        shalf[k] = (spart[k, core].astype(jnp.float32) + score[k].astype(jnp.float32)).astype(jnp.bfloat16)

    each(0, n_chip, add_cores)

    def s2(t, slot):
        return on_pair(shalf.at[t], sin.at[slot], s2_send.at[0], s2_recv.at[0], 2 * t + core)

    each(1, n_chip, lambda d: s2(wrap(chip + d, n_chip), chip).start())
    sin[chip] = shalf[chip]

    def all_g1():
        return on_pair(gin.at[1:], gin.at[1:], g1_send.at[0], g1_recv.at[0], other_core)

    def all_s2():
        return on_pair(shalf.at[1:], sin.at[1:], s2_send.at[0], s2_recv.at[0], other_core)

    all_g1().wait_recv()
    gram_ref[y, my_r, :, column(my_c)] = jnp.sum(gin[...], axis=0)

    early = lax.rem(chip, 2) == 0
    top, bottom = column(core), column(2 + core)
    mine = gram_ref.at[y, my_r, :, column(my_c)]
    tall = gram_ref.at[:, my_r, :, top]
    flat = gram_ref.at[y, :, :, bottom]

    def g2(k):
        return on_col(mine, mine, g2_send.at[0], g2_recv.at[0], half * Y + k)

    def all_g2():
        where = gram_ref.at[1:, my_r, :, top]
        return on_col(where, where, g2_send.at[0], g2_recv.at[0], (1 - half) * Y + y)

    def g3(t):
        return on_pair(tall, tall, g3_send.at[t], g3_recv.at[0], 2 * t + core)

    def h2(t):
        return on_pair(mine, mine, h2_send.at[t], h2_recv.at[0], 2 * t + core)

    def h3(k):
        return on_col(flat, flat, h3_send.at[0], h3_recv.at[0], half * Y + k)

    def all_h3():
        where = gram_ref.at[1:, :, :, bottom]
        return on_col(where, where, h3_send.at[0], h3_recv.at[0], (1 - half) * Y + y)

    def some_g3(count):
        where = gram_ref.at[:, :count, :, top]
        return on_pair(where, where, g3_send.at[0], g3_recv.at[0], other_core)

    def some_h2(count):
        where = gram_ref.at[y, :count, :, bottom]
        return on_pair(where, where, h2_send.at[0], h2_recv.at[0], other_core)

    r_tiles = n_chip // 2

    @pl.when(early)
    def _():
        each(1, Y, lambda d: g2(wrap(y + d, Y)).start())
        some_h2(r_tiles).wait_recv()
        each(1, Y, lambda d: h3(wrap(y + d, Y)).start())
        all_g2().wait_recv()
        each(1, n_chip, lambda d: g3(wrap(chip + d, n_chip)).start())

    @pl.when(jnp.logical_not(early))
    def _():
        each(1, n_chip, lambda d: h2(wrap(chip + d, n_chip)).start())
        some_h2(r_tiles - 1).wait_recv()
        each(1, Y, lambda d: h3(wrap(y + d, Y)).start())

    def s3(t):
        return on_pair(sums_ref.at[chip, core], sums_ref.at[chip, core], s3_send.at[0], s3_recv.at[0], 2 * t + core)

    def all_s3():
        where = sums_ref.at[1:, core]
        return on_pair(where, where, s3_send.at[0], s3_recv.at[0], other_core)

    def s4():
        return on_pair(sums_ref.at[:, core], sums_ref.at[:, core], s4_send.at[0], s4_recv.at[0], other_core)

    def arrived_s4():
        where = sums_ref.at[:, 1 - core]
        return on_pair(where, where, s4_send.at[0], s4_recv.at[0], other_core)

    def g4(k, lanes):
        where = gram_ref.at[:, :, :, lanes]
        return on_pair(where, where, g4_send.at[k], g4_recv.at[k], other_core)

    all_s2().wait_recv()
    sums_ref[chip, core] = jnp.sum(sin[...].astype(jnp.float32), axis=0).astype(jnp.bfloat16)
    each(1, n_chip, lambda d: s3(wrap(chip + d, n_chip)).start())

    all_h3().wait_recv()
    g4(1, bottom).start()

    @pl.when(early)
    def _():
        some_g3(r_tiles - 1).wait_recv()

    @pl.when(jnp.logical_not(early))
    def _():
        some_g3(r_tiles).wait_recv()

    g4(0, top).start()
    all_s3().wait_recv()
    s4().start()
    g4(1, column(3 - core)).wait_recv()
    g4(0, column(1 - core)).wait_recv()
    arrived_s4().wait_recv()

    for piece in range(PIECES):
        all_first(piece).wait_send()
        all_gathers(piece).wait_send()

        @pl.when(half == 0)
        def _():
            all_offers(piece).wait_send()
            across(piece).wait_send()

    all_second().wait_send()
    s1().wait_send()
    all_g1().wait_send()
    all_s2().wait_send()

    @pl.when(early)
    def _():
        all_g2().wait_send()
        each(1, n_chip, lambda d: g3(wrap(chip + d, n_chip)).wait_send())

    @pl.when(jnp.logical_not(early))
    def _():
        each(1, n_chip, lambda d: h2(wrap(chip + d, n_chip)).wait_send())

    g4(0, top).wait_send()
    g4(1, bottom).wait_send()
    all_h3().wait_send()
    all_s3().wait_send()
    s4().wait_send()


def exchange(owner, blocks, one_t):
    n_pair, s_count, _, packed, orbitals = blocks.shape
    n_chip = n_pair // 2
    width = n_pair * packed
    rows = s_count * orbitals
    chunk = 2 * width // n_pair
    vmem = pl.BlockSpec(memory_space=pltpu.VMEM)
    f32, bf16 = jnp.float32, jnp.bfloat16
    sems = []
    for send, recv in ((PIECES + 1,) * 2, (PIECES,) * 2, (PIECES,) * 2, (PIECES,) * 2, (1, 1), (1, 1), (n_chip, 1),
                       (n_chip, 1), (1, 1), (2, 2), (1, 1), (1, 1), (1, 1), (1, 1)):
        sems += [pltpu.SemaphoreType.DMA((send,)), pltpu.SemaphoreType.DMA((recv,))]
    return pl.pallas_call(
        exchange_kernel,
        out_shape=(
            jax.ShapeDtypeStruct((width, rows), bf16),
            jax.ShapeDtypeStruct((2, width, rows), bf16),
            jax.ShapeDtypeStruct((Y, width // Y // 8, 8, width), f32),
            jax.ShapeDtypeStruct((n_chip, 2, chunk, width), bf16),
        ),
        in_specs=[pl.BlockSpec(memory_space=pltpu.SMEM), vmem, vmem],
        out_specs=(vmem,) * 4,
        scratch_shapes=[
            pltpu.VMEM((2, n_pair, s_count, packed, orbitals), bf16),
            pltpu.VMEM((width, width), bf16),
            *[pltpu.VMEM((Y, width // Y, rows // PIECES), bf16)] * PIECES,
            pltpu.VMEM((width // Y, width), f32),
            pltpu.VMEM((n_pair, 8, BLOCK), f32),
            pltpu.VMEM((n_chip, 2, chunk, width), bf16),
            pltpu.VMEM((n_chip, chunk, width), bf16),
            pltpu.VMEM((n_chip, chunk, width), bf16),
            pltpu.VMEM((n_chip, chunk, width), bf16),
            *sems,
        ],
        compiler_params=pltpu.CompilerParams(collective_id=0, has_side_effects=True, vmem_limit_bytes=32 << 20),
        name="regroup_exchange",
    )(owner, blocks, one_t)


def per_device(two_rdm, one_rdm, panel_block):
    q_count, orbitals, r_count, _ = two_rdm.shape
    groups = lax.axis_size("pair")
    s_count = orbitals // groups
    panel_width = RPAN * orbitals
    col_index = lax.axis_index("col")
    first_orb = panel_block[0] * RPAN
    owner_col = first_orb // r_count
    within = first_orb % r_count
    turned = lax.dynamic_slice_in_dim(jnp.concatenate([two_rdm, two_rdm], 2), within, r_count, 2)
    blocks = jnp.transpose(turned, (3, 2, 0, 1)).reshape(groups, s_count, 2, RPAN * q_count, orbitals)
    one_cols = lax.dynamic_slice_in_dim(one_rdm, col_index * r_count, r_count, 1)
    one_t = lax.dynamic_slice_in_dim(jnp.concatenate([one_cols, one_cols], 1), within, r_count, 1).T
    panel_t, tile_t, gram, sums_t = exchange(owner_col[None], blocks, one_t)
    starts = col_index * r_count + jnp.arange(2, dtype=jnp.int32) * RPAN
    place = (jnp.arange(2, dtype=jnp.int32) + within // RPAN) % 2
    flags = jnp.concatenate([(starts >= first_orb + RPAN).astype(jnp.int32), place])
    sums_t = sums_t.reshape(2, panel_width, panel_width)
    triangle, updated = finish(
        flags, gram.reshape(panel_width, panel_width), sums_t, panel_t, tile_t, s_count, orbitals)
    return updated, triangle


def solution(mesh):
    return jax.shard_map(
        per_device,
        mesh=mesh,
        in_specs=(P("pair", None, "col", None), P(), P()),
        out_specs=(P("pair", None, "col", None), P()),
        check_vma=False,
    )
```

```python
import functools

import jax
import jax.numpy as jnp
from jax import lax
from jax.experimental import pallas as pl
from jax.experimental.pallas import tpu as pltpu
from jax.sharding import PartitionSpec as P

RPAN = 4
BLOCK = 128
STRIP = 8
EXACT = lax.Precision.HIGHEST
MESH = pl.DeviceIdType.MESH
PIECES = 2
Y = 8


def factor_block(work):
    for k in range(0, BLOCK, STRIP):
        tiles = (BLOCK - k) // STRIP
        left = work[k:BLOCK, 0:BLOCK]
        cols = [
            jnp.broadcast_to(left[:, k + j : k + j + 1], (BLOCK - k, BLOCK)).reshape(tiles, STRIP, BLOCK)
            for j in range(STRIP)
        ]
        rows_a = [jnp.broadcast_to(work[k + j : k + j + 1, :BLOCK], (STRIP, BLOCK)) for j in range(STRIP)]
        rows_b = [jnp.broadcast_to(work[k + j : k + j + 1, BLOCK:], (STRIP, BLOCK)) for j in range(STRIP)]
        entry = {
            (i, j): jnp.broadcast_to(cols[j][0, i : i + 1, :], (STRIP, BLOCK)) for j in range(STRIP) for i in range(j, STRIP)
        }
        for j in range(STRIP):
            inv = lax.rsqrt(entry[j, j])
            rows_a[j] = rows_a[j] * inv
            rows_b[j] = rows_b[j] * inv
            cols[j] = cols[j] * inv[None]
            low = {i: entry[i, j] * inv for i in range(j + 1, STRIP)}
            for i in range(j + 1, STRIP):
                for m in range(j + 1, i + 1):
                    entry[i, m] = entry[i, m] - low[i] * low[m]
                rows_a[i] = rows_a[i] - low[i] * rows_a[j]
                rows_b[i] = rows_b[i] - low[i] * rows_b[j]
                cols[i] = cols[i] - low[i][None] * cols[j]
        for j in range(STRIP):
            work[k + j : k + j + 1, :BLOCK] = rows_a[j][0:1]
            work[k + j : k + j + 1, BLOCK:] = rows_b[j][0:1]
        if tiles > 1:
            delta_a, delta_b = 0.0, 0.0
            for j in range(STRIP):
                delta_a = delta_a + cols[j][1:] * rows_a[j][None]
                delta_b = delta_b + cols[j][1:] * rows_b[j][None]
            below = BLOCK - k - STRIP
            work[k + STRIP : BLOCK, :BLOCK] = work[k + STRIP : BLOCK, :BLOCK] - delta_a.reshape(below, BLOCK)
            work[k + STRIP : BLOCK, BLOCK:] = work[k + STRIP : BLOCK, BLOCK:] - delta_b.reshape(below, BLOCK)


def finish_kernel(scale, flag_ref, gram_ref, sums_ref, panel_ref, tile_ref, tri_ref, out_ref,
                  left, right, work, basis, weights, outer):
    n = gram_ref.shape[0]
    eye = (
        lax.broadcasted_iota(jnp.int32, (BLOCK, BLOCK), 0) == lax.broadcasted_iota(jnp.int32, (BLOCK, BLOCK), 1)
    ).astype(jnp.float32)
    lower = lax.broadcasted_iota(jnp.int32, (BLOCK, BLOCK), 0) >= lax.broadcasted_iota(jnp.int32, (BLOCK, BLOCK), 1)
    upper = lax.broadcasted_iota(jnp.int32, (BLOCK, BLOCK), 0) <= lax.broadcasted_iota(jnp.int32, (BLOCK, BLOCK), 1)

    def times(a, b, dims):
        return lax.dot_general(a, b, (dims, ((), ())), preferred_element_type=jnp.float32)

    def exact(a, b, contract):
        return lax.dot_general(a, b, (((contract,), (0,)), ((), ())), precision=EXACT, preferred_element_type=jnp.float32)

    left[...] = gram_ref[...]
    right[...] = jnp.zeros((n, n), jnp.float32)
    for o in range(0, n, BLOCK):
        end = o + BLOCK
        here = work.at[o // BLOCK]
        here[:, :BLOCK] = left[o:end, o:end]
        here[:, BLOCK:] = eye
        factor_block(here)
        invert = jnp.where(lower, here[:, BLOCK:], 0.0)
        right[o:end, o:end] = invert
        if o:
            right[o:end, :o] = exact(invert, right[o:end, :o], 1)
            tri_ref[o:end, :o] = jnp.zeros((BLOCK, o), jnp.float32)
        tri_ref[o:end, o:end] = jnp.where(upper, here[:, :BLOCK], 0.0) / scale
        if end < n:
            left[o:end, end:] = exact(invert, left[o:end, end:], 1)
            tri_ref[o:end, end:] = left[o:end, end:] / scale
            for q in range(end, n, BLOCK):
                u = left[o:end, q:q + BLOCK]
                left[q:q + BLOCK, q:] = left[q:q + BLOCK, q:] - exact(u, left[o:end, q:], 0)
                right[q:q + BLOCK, :end] = right[q:q + BLOCK, :end] - exact(u, right[o:end, :end], 0)
        inverse = right[o:end, :end]
        high = inverse.astype(jnp.bfloat16)
        low = (inverse - high.astype(jnp.float32)).astype(jnp.bfloat16)
        basis[o:end] = (
            times(high, panel_ref[:end], ((1,), (0,))) + times(low, panel_ref[:end], ((1,), (0,)))
        ).astype(jnp.bfloat16)
        for h in range(2):
            sums = sums_ref[h, :, :end]
            weights[h, :, o:end] = (times(sums, high, ((1,), (1,))) + times(sums, low, ((1,), (1,)))).astype(jnp.bfloat16)

    s_count, orbitals, r_count, _ = out_ref.shape
    per_half = r_count // 2
    for h in range(2):
        source = flag_ref[2 + h]
        product = times(weights[source], basis[...], ((1,), (0,)))
        outer[h] = tile_ref[source].astype(jnp.float32) - jnp.where(flag_ref[h] > 0, product, 0.0)
    for s in range(s_count):
        parts = [
            outer[h, r * BLOCK:(r + 1) * BLOCK, s * orbitals:(s + 1) * orbitals].T
            for h in range(2) for r in range(per_half)
        ]
        out_ref[s] = jnp.stack(parts, axis=1).astype(jnp.bfloat16)


def finish(flags, gram, sums, panel_t, tile_t, s_count, scale):
    n = gram.shape[0]
    rows = panel_t.shape[1]
    whole = pl.BlockSpec(memory_space=pltpu.VMEM)
    return pl.pallas_call(
        functools.partial(finish_kernel, scale),
        out_shape=(
            jax.ShapeDtypeStruct((n, n), jnp.float32),
            jax.ShapeDtypeStruct((s_count, rows // s_count, 2 * n // BLOCK, BLOCK), jnp.bfloat16),
        ),
        in_specs=[pl.BlockSpec(memory_space=pltpu.SMEM)] + [whole] * 4,
        out_specs=(whole,) * 2,
        scratch_shapes=[
            pltpu.VMEM((n, n), jnp.float32),
            pltpu.VMEM((n, n), jnp.float32),
            pltpu.VMEM((n // BLOCK, BLOCK, 2 * BLOCK), jnp.float32),
            pltpu.VMEM((n, rows), jnp.bfloat16),
            pltpu.VMEM((2, n, n), jnp.bfloat16),
            pltpu.VMEM((2, n, rows), jnp.float32),
        ],
        compiler_params=pltpu.CompilerParams(vmem_limit_bytes=32 << 20),
        cost_estimate=pl.CostEstimate(flops=16 * n**3, bytes_accessed=24 * n * n, transcendentals=n),
        name="factor_apply",
    )(flags, gram, sums, panel_t, tile_t)


def wrap(value, count):
    return jnp.where(value >= count, value - count, value)


def each(start, stop, body):
    lax.fori_loop(start, stop, lambda k, c: (body(k), c)[1], 0)


def exchange_kernel(owner_ref, x_ref, one_ref, panel_ref, gt_ref, gram_ref, sums_ref,
                    land, order, picks_a, picks_b, gpart, gin, spart, score, shalf, sin,
                    a_send, a_recv, p_send, p_recv, q_send, q_recv, c_send, c_recv, g1_send, g1_recv, g2_send, g2_recv,
                    g3_send, g3_recv, h2_send, h2_recv, h3_send, h3_recv, g4_send, g4_recv,
                    s1_send, s1_recv, s2_send, s2_recv, s3_send, s3_recv, s4_send, s4_recv):
    pair = lax.axis_index("pair")
    colm = lax.axis_index("col")
    n_pair = lax.axis_size("pair")
    n_chip = n_pair // 2
    chip, core = pair // 2, lax.rem(pair, 2)
    half, y = colm // Y, lax.rem(colm, Y)
    other_core = 2 * chip + 1 - core
    width = panel_ref.shape[0]
    part = width // Y
    wide = width // BLOCK
    s_count = x_ref.shape[1]
    s_piece = s_count // PIECES
    over_last = (((1,), (1,)), ((), ()))
    picks = (picks_a, picks_b)

    def on_pair(src, dst, send, recv, k):
        return pltpu.make_async_remote_copy(
            src_ref=src, dst_ref=dst, send_sem=send, recv_sem=recv, device_id={"pair": k}, device_id_type=MESH)

    def on_col(src, dst, send, recv, k):
        return pltpu.make_async_remote_copy(
            src_ref=src, dst_ref=dst, send_sem=send, recv_sem=recv, device_id={"col": k}, device_id_type=MESH)

    barrier = pltpu.get_barrier_semaphore()
    each(1, n_pair, lambda d: pl.semaphore_signal(
        barrier, inc=1, device_id={"pair": wrap(pair + d, n_pair)}, device_id_type=MESH))
    each(1, Y, lambda d: pl.semaphore_signal(
        barrier, inc=1, device_id={"col": half * Y + wrap(y + d, Y)}, device_id_type=MESH))
    pl.semaphore_signal(barrier, inc=1, device_id={"col": (1 - half) * Y + y}, device_id_type=MESH)
    pl.semaphore_wait(barrier, n_pair + Y - 1)

    def first(k, peer, slot):
        ss = pl.ds(k * s_piece, s_piece)
        return on_pair(x_ref.at[peer, ss, 0], land.at[0, slot, ss], a_send.at[k], a_recv.at[k], peer)

    def second(peer, slot):
        return on_pair(x_ref.at[peer, :, 1], land.at[1, slot], a_send.at[PIECES], a_recv.at[PIECES], peer)

    def all_first(k):
        ss = pl.ds(k * s_piece, s_piece)
        return on_pair(x_ref.at[1:, ss, 0], land.at[0, 1:, ss], a_send.at[k], a_recv.at[k], other_core)

    def all_second():
        return on_pair(x_ref.at[1:, :, 1], land.at[1, 1:], a_send.at[PIECES], a_recv.at[PIECES], other_core)

    for k in range(PIECES):
        each(1, n_pair, lambda d: first(k, wrap(pair + d, n_pair), pair).start())
    for h in range(2):
        land[h, pair] = x_ref[pair, :, h]

    row = lax.broadcasted_iota(jnp.int32, (width, width), 0)
    col = lax.broadcasted_iota(jnp.int32, (width, width), 1)
    q, r = row & (BLOCK - 1), row // BLOCK
    order[...] = (col == (q // 4) * 16 + r * 4 + (q & 3)).astype(jnp.float32).astype(jnp.bfloat16)
    q_row = lax.broadcasted_iota(jnp.int32, (BLOCK, BLOCK), 0)

    def build(h, s):
        moved = land[h, :, s].reshape(width, BLOCK)
        placed = jnp.dot(order[...], moved, preferred_element_type=jnp.float32)
        for r in range(wide):
            diagonal = jnp.where(q_row == pair * s_count + s, one_ref[pl.ds(h * wide + r, 1), :], 0.0)
            gt_ref[h, r * BLOCK:(r + 1) * BLOCK, s * BLOCK:(s + 1) * BLOCK] = (
                diagonal - placed[r * BLOCK:(r + 1) * BLOCK]).astype(jnp.bfloat16)

    span = s_piece * BLOCK

    def block(k, piece):
        return pl.ds(pl.multiple_of(k * part, part), part), pl.ds(piece * span, span)

    def offer(piece, k, slot):
        rows, lanes = block(k, piece)
        return on_col(gt_ref.at[0, rows, lanes], picks[piece].at[slot], p_send.at[piece], p_recv.at[piece], k)

    def across(piece):
        where = panel_ref.at[block(y, piece)]
        return on_col(where, where, q_send.at[piece], q_recv.at[piece], (1 - half) * Y + y)

    def gather(piece, k, row):
        where = panel_ref.at[block(row, piece)]
        return on_col(where, where, c_send.at[piece], c_recv.at[piece], half * Y + k)

    def all_offers(piece):
        lanes = pl.ds(piece * span, span)
        return on_col(gt_ref.at[0, :(Y - 1) * part, lanes], picks[piece].at[1:], p_send.at[piece], p_recv.at[piece],
                      (1 - half) * Y + y)

    def all_gathers(piece):
        where = panel_ref.at[:(Y - 1) * part, pl.ds(piece * span, span)]
        return on_col(where, where, c_send.at[piece], c_recv.at[piece], (1 - half) * Y + y)

    for piece in range(PIECES):
        all_first(piece).wait_recv()
        for s in range(piece * s_piece, (piece + 1) * s_piece):
            build(0, s)

        @pl.when(half == 0)
        def _():
            each(1, Y, lambda d: offer(piece, wrap(y + d, Y), y).start())
            rows, lanes = block(y, piece)
            picks[piece][y] = gt_ref[0, rows, lanes]

    each(1, n_pair, lambda d: second(wrap(pair + d, n_pair), pair).start())

    for piece in range(PIECES):
        @pl.when(half == 0)
        def _():
            all_offers(piece).wait_recv()
            rows, lanes = block(y, piece)
            panel_ref[rows, lanes] = picks[piece][owner_ref[0]]
            across(piece).start()

        @pl.when(half == 1)
        def _():
            across(piece).wait_recv()

        each(1, Y, lambda d: gather(piece, wrap(y + d, Y), y).start())

    all_second().wait_recv()
    for s in range(s_count):
        build(1, s)
    for piece in range(PIECES):
        all_gathers(piece).wait_recv()

    chunk = sums_ref.shape[2]
    rows_at_once = 2 * BLOCK
    count = rows_at_once // (2 * chunk)
    for h in range(2):
        for k in range(width // rows_at_once):
            out = lax.dot_general(gt_ref[h, k * rows_at_once:(k + 1) * rows_at_once, :], panel_ref[...], over_last,
                                  preferred_element_type=jnp.float32).astype(jnp.bfloat16)
            at = (h * (width // rows_at_once) + k) * count
            spart[at:at + count] = out.reshape(count, 2, chunk, width)

    def s1():
        return on_pair(spart.at[:, 1 - core], score, s1_send.at[0], s1_recv.at[0], other_core)

    s1().start()

    gpart[...] = lax.dot_general(panel_ref[pl.ds(pl.multiple_of(y * part, part), part), :], panel_ref[...], over_last,
                                 preferred_element_type=jnp.float32)

    def column(c):
        return pl.ds(pl.multiple_of(c * BLOCK, BLOCK), BLOCK)

    def g1(i, slot):
        src = gpart.at[pl.ds(pl.multiple_of((i // wide) * 8, 8), 8), column(lax.rem(i, wide))]
        return on_pair(src, gin.at[slot], g1_send.at[0], g1_recv.at[0], i)

    each(1, n_pair, lambda d: g1(wrap(pair + d, n_pair), pair).start())
    my_r, my_c = pair // wide, lax.rem(pair, wide)
    gin[pair] = gpart[pl.ds(pl.multiple_of(my_r * 8, 8), 8), column(my_c)]

    s1().wait_recv()

    def add_cores(k):
        shalf[k] = (spart[k, core].astype(jnp.float32) + score[k].astype(jnp.float32)).astype(jnp.bfloat16)

    each(0, n_chip, add_cores)

    def s2(t, slot):
        return on_pair(shalf.at[t], sin.at[slot], s2_send.at[0], s2_recv.at[0], 2 * t + core)

    each(1, n_chip, lambda d: s2(wrap(chip + d, n_chip), chip).start())
    sin[chip] = shalf[chip]

    def all_g1():
        return on_pair(gin.at[1:], gin.at[1:], g1_send.at[0], g1_recv.at[0], other_core)

    def all_s2():
        return on_pair(shalf.at[1:], sin.at[1:], s2_send.at[0], s2_recv.at[0], other_core)

    all_g1().wait_recv()
    gram_ref[y, my_r, :, column(my_c)] = jnp.sum(gin[...], axis=0)

    early = lax.rem(chip, 2) == 0
    top, bottom = column(core), column(2 + core)
    mine = gram_ref.at[y, my_r, :, column(my_c)]
    tall = gram_ref.at[:, my_r, :, top]
    flat = gram_ref.at[y, :, :, bottom]

    def g2(k):
        return on_col(mine, mine, g2_send.at[0], g2_recv.at[0], half * Y + k)

    def all_g2():
        where = gram_ref.at[1:, my_r, :, top]
        return on_col(where, where, g2_send.at[0], g2_recv.at[0], (1 - half) * Y + y)

    def g3(t):
        return on_pair(tall, tall, g3_send.at[t], g3_recv.at[0], 2 * t + core)

    def h2(t):
        return on_pair(mine, mine, h2_send.at[t], h2_recv.at[0], 2 * t + core)

    def h3(k):
        return on_col(flat, flat, h3_send.at[0], h3_recv.at[0], half * Y + k)

    def all_h3():
        where = gram_ref.at[1:, :, :, bottom]
        return on_col(where, where, h3_send.at[0], h3_recv.at[0], (1 - half) * Y + y)

    def some_g3(count):
        where = gram_ref.at[:, :count, :, top]
        return on_pair(where, where, g3_send.at[0], g3_recv.at[0], other_core)

    def some_h2(count):
        where = gram_ref.at[y, :count, :, bottom]
        return on_pair(where, where, h2_send.at[0], h2_recv.at[0], other_core)

    r_tiles = n_chip // 2

    @pl.when(early)
    def _():
        each(1, Y, lambda d: g2(wrap(y + d, Y)).start())
        some_h2(r_tiles).wait_recv()
        each(1, Y, lambda d: h3(wrap(y + d, Y)).start())
        all_g2().wait_recv()
        each(1, n_chip, lambda d: g3(wrap(chip + d, n_chip)).start())

    @pl.when(jnp.logical_not(early))
    def _():
        each(1, n_chip, lambda d: h2(wrap(chip + d, n_chip)).start())
        some_h2(r_tiles - 1).wait_recv()
        each(1, Y, lambda d: h3(wrap(y + d, Y)).start())

    def s3(t):
        return on_pair(sums_ref.at[chip, core], sums_ref.at[chip, core], s3_send.at[0], s3_recv.at[0], 2 * t + core)

    def all_s3():
        where = sums_ref.at[1:, core]
        return on_pair(where, where, s3_send.at[0], s3_recv.at[0], other_core)

    def s4():
        return on_pair(sums_ref.at[:, core], sums_ref.at[:, core], s4_send.at[0], s4_recv.at[0], other_core)

    def arrived_s4():
        where = sums_ref.at[:, 1 - core]
        return on_pair(where, where, s4_send.at[0], s4_recv.at[0], other_core)

    def g4(k, lanes):
        where = gram_ref.at[:, :, :, lanes]
        return on_pair(where, where, g4_send.at[k], g4_recv.at[k], other_core)

    all_s2().wait_recv()
    sums_ref[chip, core] = jnp.sum(sin[...].astype(jnp.float32), axis=0).astype(jnp.bfloat16)
    each(1, n_chip, lambda d: s3(wrap(chip + d, n_chip)).start())

    all_h3().wait_recv()
    g4(1, bottom).start()

    @pl.when(early)
    def _():
        some_g3(r_tiles - 1).wait_recv()

    @pl.when(jnp.logical_not(early))
    def _():
        some_g3(r_tiles).wait_recv()

    g4(0, top).start()
    all_s3().wait_recv()
    s4().start()
    g4(1, column(3 - core)).wait_recv()
    g4(0, column(1 - core)).wait_recv()
    arrived_s4().wait_recv()

    for piece in range(PIECES):
        all_first(piece).wait_send()
        all_gathers(piece).wait_send()

        @pl.when(half == 0)
        def _():
            all_offers(piece).wait_send()
            across(piece).wait_send()

    all_second().wait_send()
    s1().wait_send()
    all_g1().wait_send()
    all_s2().wait_send()

    @pl.when(early)
    def _():
        all_g2().wait_send()
        each(1, n_chip, lambda d: g3(wrap(chip + d, n_chip)).wait_send())

    @pl.when(jnp.logical_not(early))
    def _():
        each(1, n_chip, lambda d: h2(wrap(chip + d, n_chip)).wait_send())

    g4(0, top).wait_send()
    g4(1, bottom).wait_send()
    all_h3().wait_send()
    all_s3().wait_send()
    s4().wait_send()


def exchange(owner, blocks, one_t):
    n_pair, s_count, _, packed, orbitals = blocks.shape
    n_chip = n_pair // 2
    width = n_pair * packed
    rows = s_count * orbitals
    chunk = 2 * width // n_pair
    vmem = pl.BlockSpec(memory_space=pltpu.VMEM)
    f32, bf16 = jnp.float32, jnp.bfloat16
    sems = []
    for send, recv in ((PIECES + 1,) * 2, (PIECES,) * 2, (PIECES,) * 2, (PIECES,) * 2, (1, 1), (1, 1), (n_chip, 1),
                       (n_chip, 1), (1, 1), (2, 2), (1, 1), (1, 1), (1, 1), (1, 1)):
        sems += [pltpu.SemaphoreType.DMA((send,)), pltpu.SemaphoreType.DMA((recv,))]
    return pl.pallas_call(
        exchange_kernel,
        out_shape=(
            jax.ShapeDtypeStruct((width, rows), bf16),
            jax.ShapeDtypeStruct((2, width, rows), bf16),
            jax.ShapeDtypeStruct((Y, width // Y // 8, 8, width), f32),
            jax.ShapeDtypeStruct((n_chip, 2, chunk, width), bf16),
        ),
        in_specs=[pl.BlockSpec(memory_space=pltpu.SMEM), vmem, vmem],
        out_specs=(vmem,) * 4,
        scratch_shapes=[
            pltpu.VMEM((2, n_pair, s_count, packed, orbitals), bf16),
            pltpu.VMEM((width, width), bf16),
            *[pltpu.VMEM((Y, width // Y, rows // PIECES), bf16)] * PIECES,
            pltpu.VMEM((width // Y, width), f32),
            pltpu.VMEM((n_pair, 8, BLOCK), f32),
            pltpu.VMEM((n_chip, 2, chunk, width), bf16),
            pltpu.VMEM((n_chip, chunk, width), bf16),
            pltpu.VMEM((n_chip, chunk, width), bf16),
            pltpu.VMEM((n_chip, chunk, width), bf16),
            *sems,
        ],
        compiler_params=pltpu.CompilerParams(collective_id=0, has_side_effects=True, vmem_limit_bytes=32 << 20),
        name="regroup_exchange",
    )(owner, blocks, one_t)


def per_device(two_rdm, one_rdm, panel_block):
    q_count, orbitals, r_count, _ = two_rdm.shape
    groups = lax.axis_size("pair")
    s_count = orbitals // groups
    panel_width = RPAN * orbitals
    col_index = lax.axis_index("col")
    first_orb = panel_block[0] * RPAN
    owner_col = first_orb // r_count
    within = first_orb % r_count
    turned = lax.dynamic_slice_in_dim(jnp.concatenate([two_rdm, two_rdm], 2), within, r_count, 2)
    blocks = jnp.transpose(turned, (3, 2, 0, 1)).reshape(groups, s_count, 2, RPAN * q_count, orbitals)
    one_cols = lax.dynamic_slice_in_dim(one_rdm, col_index * r_count, r_count, 1)
    one_t = lax.dynamic_slice_in_dim(jnp.concatenate([one_cols, one_cols], 1), within, r_count, 1).T
    panel_t, tile_t, gram, sums_t = exchange(owner_col[None], blocks, one_t)
    starts = col_index * r_count + jnp.arange(2, dtype=jnp.int32) * RPAN
    place = (jnp.arange(2, dtype=jnp.int32) + within // RPAN) % 2
    flags = jnp.concatenate([(starts >= first_orb + RPAN).astype(jnp.int32), place])
    sums_t = sums_t.reshape(2, panel_width, panel_width)
    triangle, updated = finish(
        flags, gram.reshape(panel_width, panel_width), sums_t, panel_t, tile_t, s_count, orbitals)
    return updated, triangle


def solution(mesh):
    return jax.shard_map(
        per_device,
        mesh=mesh,
        in_specs=(P("pair", None, "col", None), P(), P()),
        out_specs=(P("pair", None, "col", None), P()),
        check_vma=False,
    )
```

```python
import functools

import jax
import jax.numpy as jnp
from jax import lax
from jax.experimental import pallas as pl
from jax.experimental.pallas import tpu as pltpu
from jax.sharding import PartitionSpec as P

RPAN = 4
BLOCK = 128
STRIP = 8
EXACT = lax.Precision.HIGHEST
MESH = pl.DeviceIdType.MESH
Y = 8


def factor_block(work):
    for k in range(0, BLOCK, STRIP):
        tiles = (BLOCK - k) // STRIP
        left = work[k:BLOCK, 0:BLOCK]
        cols = [
            jnp.broadcast_to(left[:, k + j : k + j + 1], (BLOCK - k, BLOCK)).reshape(tiles, STRIP, BLOCK)
            for j in range(STRIP)
        ]
        rows_a = [jnp.broadcast_to(work[k + j : k + j + 1, :BLOCK], (STRIP, BLOCK)) for j in range(STRIP)]
        rows_b = [jnp.broadcast_to(work[k + j : k + j + 1, BLOCK:], (STRIP, BLOCK)) for j in range(STRIP)]
        entry = {
            (i, j): jnp.broadcast_to(cols[j][0, i : i + 1, :], (STRIP, BLOCK)) for j in range(STRIP) for i in range(j, STRIP)
        }
        for j in range(STRIP):
            inv = lax.rsqrt(entry[j, j])
            rows_a[j] = rows_a[j] * inv
            rows_b[j] = rows_b[j] * inv
            cols[j] = cols[j] * inv[None]
            low = {i: entry[i, j] * inv for i in range(j + 1, STRIP)}
            for i in range(j + 1, STRIP):
                for m in range(j + 1, i + 1):
                    entry[i, m] = entry[i, m] - low[i] * low[m]
                rows_a[i] = rows_a[i] - low[i] * rows_a[j]
                rows_b[i] = rows_b[i] - low[i] * rows_b[j]
                cols[i] = cols[i] - low[i][None] * cols[j]
        for j in range(STRIP):
            work[k + j : k + j + 1, :BLOCK] = rows_a[j][0:1]
            work[k + j : k + j + 1, BLOCK:] = rows_b[j][0:1]
        if tiles > 1:
            delta_a, delta_b = 0.0, 0.0
            for j in range(STRIP):
                delta_a = delta_a + cols[j][1:] * rows_a[j][None]
                delta_b = delta_b + cols[j][1:] * rows_b[j][None]
            below = BLOCK - k - STRIP
            work[k + STRIP : BLOCK, :BLOCK] = work[k + STRIP : BLOCK, :BLOCK] - delta_a.reshape(below, BLOCK)
            work[k + STRIP : BLOCK, BLOCK:] = work[k + STRIP : BLOCK, BLOCK:] - delta_b.reshape(below, BLOCK)


def finish_kernel(scale, flag_ref, gram_ref, sums_ref, panel_ref, tile_ref, tri_ref, out_ref,
                  left, right, work, basis, weights, outer):
    n = gram_ref.shape[0]
    eye = (
        lax.broadcasted_iota(jnp.int32, (BLOCK, BLOCK), 0) == lax.broadcasted_iota(jnp.int32, (BLOCK, BLOCK), 1)
    ).astype(jnp.float32)
    lower = lax.broadcasted_iota(jnp.int32, (BLOCK, BLOCK), 0) >= lax.broadcasted_iota(jnp.int32, (BLOCK, BLOCK), 1)
    upper = lax.broadcasted_iota(jnp.int32, (BLOCK, BLOCK), 0) <= lax.broadcasted_iota(jnp.int32, (BLOCK, BLOCK), 1)

    def times(a, b, dims):
        return lax.dot_general(a, b, (dims, ((), ())), preferred_element_type=jnp.float32)

    def exact(a, b, contract):
        return lax.dot_general(a, b, (((contract,), (0,)), ((), ())), precision=EXACT, preferred_element_type=jnp.float32)

    left[...] = gram_ref[...]
    right[...] = jnp.zeros((n, n), jnp.float32)
    for o in range(0, n, BLOCK):
        end = o + BLOCK
        here = work.at[o // BLOCK]
        here[:, :BLOCK] = left[o:end, o:end]
        here[:, BLOCK:] = eye
        factor_block(here)
        invert = jnp.where(lower, here[:, BLOCK:], 0.0)
        right[o:end, o:end] = invert
        if o:
            right[o:end, :o] = exact(invert, right[o:end, :o], 1)
            tri_ref[o:end, :o] = jnp.zeros((BLOCK, o), jnp.float32)
        tri_ref[o:end, o:end] = jnp.where(upper, here[:, :BLOCK], 0.0) / scale
        if end < n:
            left[o:end, end:] = exact(invert, left[o:end, end:], 1)
            tri_ref[o:end, end:] = left[o:end, end:] / scale
            for q in range(end, n, BLOCK):
                u = left[o:end, q:q + BLOCK]
                left[q:q + BLOCK, q:] = left[q:q + BLOCK, q:] - exact(u, left[o:end, q:], 0)
                right[q:q + BLOCK, :end] = right[q:q + BLOCK, :end] - exact(u, right[o:end, :end], 0)
        inverse = right[o:end, :end]
        high = inverse.astype(jnp.bfloat16)
        low = (inverse - high.astype(jnp.float32)).astype(jnp.bfloat16)
        basis[o:end] = (
            times(high, panel_ref[:end], ((1,), (0,))) + times(low, panel_ref[:end], ((1,), (0,)))
        ).astype(jnp.bfloat16)
        for h in range(2):
            sums = sums_ref[h, :, :end]
            weights[h, :, o:end] = (times(sums, high, ((1,), (1,))) + times(sums, low, ((1,), (1,)))).astype(jnp.bfloat16)

    s_count, orbitals, r_count, _ = out_ref.shape
    per_half = r_count // 2
    for h in range(2):
        source = flag_ref[2 + h]
        product = times(weights[source], basis[...], ((1,), (0,)))
        outer[h] = tile_ref[source].astype(jnp.float32) - jnp.where(flag_ref[h] > 0, product, 0.0)
    for s in range(s_count):
        parts = [
            outer[h, r * BLOCK:(r + 1) * BLOCK, s * orbitals:(s + 1) * orbitals].T
            for h in range(2) for r in range(per_half)
        ]
        out_ref[s] = jnp.stack(parts, axis=1).astype(jnp.bfloat16)


def finish(flags, gram, sums, panel_t, tile_t, s_count, scale):
    n = gram.shape[0]
    rows = panel_t.shape[1]
    whole = pl.BlockSpec(memory_space=pltpu.VMEM)
    return pl.pallas_call(
        functools.partial(finish_kernel, scale),
        out_shape=(
            jax.ShapeDtypeStruct((n, n), jnp.float32),
            jax.ShapeDtypeStruct((s_count, rows // s_count, 2 * n // BLOCK, BLOCK), jnp.bfloat16),
        ),
        in_specs=[pl.BlockSpec(memory_space=pltpu.SMEM)] + [whole] * 4,
        out_specs=(whole,) * 2,
        scratch_shapes=[
            pltpu.VMEM((n, n), jnp.float32),
            pltpu.VMEM((n, n), jnp.float32),
            pltpu.VMEM((n // BLOCK, BLOCK, 2 * BLOCK), jnp.float32),
            pltpu.VMEM((n, rows), jnp.bfloat16),
            pltpu.VMEM((2, n, n), jnp.bfloat16),
            pltpu.VMEM((2, n, rows), jnp.float32),
        ],
        compiler_params=pltpu.CompilerParams(vmem_limit_bytes=32 << 20),
        cost_estimate=pl.CostEstimate(flops=16 * n**3, bytes_accessed=24 * n * n, transcendentals=n),
        name="factor_apply",
    )(flags, gram, sums, panel_t, tile_t)


def wrap(value, count):
    return jnp.where(value >= count, value - count, value)


def each(start, stop, body):
    lax.fori_loop(start, stop, lambda k, c: (body(k), c)[1], 0)


def exchange_kernel(owner_ref, x_ref, one_ref, one_panel_ref, panel_ref, gt_ref, gram_ref, sums_ref,
                    land, order, picks, chosen, raw, gpart, gin, spart, score, shalf, sin,
                    a_send, a_recv, p_send, p_recv, q_send, q_recv, m_send, m_recv, c_send, c_recv,
                    g1_send, g1_recv, g2_send, g2_recv,
                    g3_send, g3_recv, h2_send, h2_recv, h3_send, h3_recv, g4_send, g4_recv,
                    s1_send, s1_recv, s2_send, s2_recv, s3_send, s3_recv, s4_send, s4_recv):
    pair = lax.axis_index("pair")
    colm = lax.axis_index("col")
    n_pair = lax.axis_size("pair")
    n_chip = n_pair // 2
    chip, core = pair // 2, lax.rem(pair, 2)
    half, y = colm // Y, lax.rem(colm, Y)
    other_core = 2 * chip + 1 - core
    width = panel_ref.shape[0]
    part = width // Y
    wide = width // BLOCK
    s_count = x_ref.shape[1]
    over_last = (((1,), (1,)), ((), ()))

    def on_pair(src, dst, send, recv, k):
        return pltpu.make_async_remote_copy(
            src_ref=src, dst_ref=dst, send_sem=send, recv_sem=recv, device_id={"pair": k}, device_id_type=MESH)

    def on_col(src, dst, send, recv, k):
        return pltpu.make_async_remote_copy(
            src_ref=src, dst_ref=dst, send_sem=send, recv_sem=recv, device_id={"col": k}, device_id_type=MESH)

    barrier = pltpu.get_barrier_semaphore()
    each(1, n_pair, lambda d: pl.semaphore_signal(
        barrier, inc=1, device_id={"pair": wrap(pair + d, n_pair)}, device_id_type=MESH))
    each(1, Y, lambda d: pl.semaphore_signal(
        barrier, inc=1, device_id={"col": half * Y + wrap(y + d, Y)}, device_id_type=MESH))
    pl.semaphore_signal(barrier, inc=1, device_id={"col": (1 - half) * Y + y}, device_id_type=MESH)
    pl.semaphore_wait(barrier, n_pair + Y - 1)

    def offer(k):
        return on_col(x_ref.at[:, k // 2, 0, lax.rem(k, 2)], picks.at[y], p_send.at[0], p_recv.at[0], k)

    def all_offers():
        return on_col(picks.at[1:], picks.at[1:], p_send.at[0], p_recv.at[0], (1 - half) * Y + y)

    @pl.when(half == 0)
    def _():
        each(1, Y, lambda d: offer(wrap(y + d, Y)).start())

    def block(h, peer):
        return on_pair(x_ref.at[peer, :, h], land.at[pair, :, h], a_send.at[h], a_recv.at[h], peer)

    def all_blocks(h):
        return on_pair(x_ref.at[1:, :, h], land.at[1:, :, h], a_send.at[h], a_recv.at[h], other_core)

    each(1, n_pair, lambda d: block(0, wrap(pair + d, n_pair)).start())
    land[pair] = x_ref[pair]

    size = 2 * BLOCK
    row = lax.broadcasted_iota(jnp.int32, (size, size), 0)
    col = lax.broadcasted_iota(jnp.int32, (size, size), 1)
    q, r = row & (BLOCK - 1), row // BLOCK
    order[...] = (col == (q // 4) * 8 + r * 4 + (q & 3)).astype(jnp.float32).astype(jnp.bfloat16)
    q_row = lax.broadcasted_iota(jnp.int32, (BLOCK, BLOCK), 0)

    def columns_of(moved, ones, u, s):
        placed = jnp.dot(order[...], moved.reshape(size, BLOCK), preferred_element_type=jnp.float32)
        out = []
        for v in range(2):
            diagonal = jnp.where(q_row == pair * s_count + s, ones[2 * u + v:2 * u + v + 1, :], 0.0)
            out.append(diagonal - placed[v * BLOCK:(v + 1) * BLOCK])
        return jnp.concatenate(out, axis=0).astype(jnp.bfloat16)

    def build(h):
        ones = one_ref[h * wide:(h + 1) * wide, :]
        for s in range(s_count):
            for u in range(2):
                gt_ref[h, u * size:(u + 1) * size, s * BLOCK:(s + 1) * BLOCK] = columns_of(land[:, s, h, u], ones, u, s)

    def across():
        return on_col(chosen, chosen, q_send.at[0], q_recv.at[0], (1 - half) * Y + y)

    def deal(peer):
        return on_pair(chosen.at[peer], raw.at[y, pair], m_send.at[0], m_recv.at[0], peer)

    def all_deals():
        return on_pair(raw.at[y, 1:], raw.at[y, 1:], m_send.at[0], m_recv.at[0], other_core)

    def gather(k):
        return on_col(raw.at[y], raw.at[y], c_send.at[0], c_recv.at[0], half * Y + k)

    def all_gathers():
        return on_col(raw.at[1:], raw.at[1:], c_send.at[0], c_recv.at[0], (1 - half) * Y + y)

    @pl.when(half == 0)
    def _():
        picks[y] = x_ref[:, y // 2, 0, lax.rem(y, 2)]
        all_offers().wait_recv()
        chosen[...] = picks[owner_ref[0]]
        across().start()

    @pl.when(half == 1)
    def _():
        across().wait_recv()

    each(1, n_pair, lambda d: deal(wrap(pair + d, n_pair)).start())
    raw[y, pair] = chosen[pair]
    each(1, n_pair, lambda d: block(1, wrap(pair + d, n_pair)).start())
    all_deals().wait_recv()
    each(1, Y, lambda d: gather(wrap(y + d, Y)).start())
    for h in range(2):
        all_blocks(h).wait_recv()
        build(h)
    all_gathers().wait_recv()
    for k in range(Y):
        s, u = k // 2, k % 2
        panel_ref[u * size:(u + 1) * size, s * BLOCK:(s + 1) * BLOCK] = columns_of(raw[k], one_panel_ref[...], u, s)

    chunk = sums_ref.shape[2]
    rows_at_once = 2 * BLOCK
    count = rows_at_once // (2 * chunk)
    for h in range(2):
        for k in range(width // rows_at_once):
            out = lax.dot_general(gt_ref[h, k * rows_at_once:(k + 1) * rows_at_once, :], panel_ref[...], over_last,
                                  preferred_element_type=jnp.float32).astype(jnp.bfloat16)
            at = (h * (width // rows_at_once) + k) * count
            spart[at:at + count] = out.reshape(count, 2, chunk, width)

    def s1():
        return on_pair(spart.at[:, 1 - core], score, s1_send.at[0], s1_recv.at[0], other_core)

    s1().start()

    gpart[...] = lax.dot_general(panel_ref[pl.ds(pl.multiple_of(y * part, part), part), :], panel_ref[...], over_last,
                                 preferred_element_type=jnp.float32)

    def column(c):
        return pl.ds(pl.multiple_of(c * BLOCK, BLOCK), BLOCK)

    def g1(i, slot):
        src = gpart.at[pl.ds(pl.multiple_of((i // wide) * 8, 8), 8), column(lax.rem(i, wide))]
        return on_pair(src, gin.at[slot], g1_send.at[0], g1_recv.at[0], i)

    each(1, n_pair, lambda d: g1(wrap(pair + d, n_pair), pair).start())
    my_r, my_c = pair // wide, lax.rem(pair, wide)
    gin[pair] = gpart[pl.ds(pl.multiple_of(my_r * 8, 8), 8), column(my_c)]

    s1().wait_recv()

    def add_cores(k):
        shalf[k] = (spart[k, core].astype(jnp.float32) + score[k].astype(jnp.float32)).astype(jnp.bfloat16)

    each(0, n_chip, add_cores)

    def s2(t, slot):
        return on_pair(shalf.at[t], sin.at[slot], s2_send.at[0], s2_recv.at[0], 2 * t + core)

    each(1, n_chip, lambda d: s2(wrap(chip + d, n_chip), chip).start())
    sin[chip] = shalf[chip]

    def all_g1():
        return on_pair(gin.at[1:], gin.at[1:], g1_send.at[0], g1_recv.at[0], other_core)

    def all_s2():
        return on_pair(shalf.at[1:], sin.at[1:], s2_send.at[0], s2_recv.at[0], other_core)

    all_g1().wait_recv()
    gram_ref[y, my_r, :, column(my_c)] = jnp.sum(gin[...], axis=0)

    early = lax.rem(chip, 2) == 0
    top, bottom = column(core), column(2 + core)
    mine = gram_ref.at[y, my_r, :, column(my_c)]
    tall = gram_ref.at[:, my_r, :, top]
    flat = gram_ref.at[y, :, :, bottom]

    def g2(k):
        return on_col(mine, mine, g2_send.at[0], g2_recv.at[0], half * Y + k)

    def all_g2():
        where = gram_ref.at[1:, my_r, :, top]
        return on_col(where, where, g2_send.at[0], g2_recv.at[0], (1 - half) * Y + y)

    def g3(t):
        return on_pair(tall, tall, g3_send.at[t], g3_recv.at[0], 2 * t + core)

    def h2(t):
        return on_pair(mine, mine, h2_send.at[t], h2_recv.at[0], 2 * t + core)

    def h3(k):
        return on_col(flat, flat, h3_send.at[0], h3_recv.at[0], half * Y + k)

    def all_h3():
        where = gram_ref.at[1:, :, :, bottom]
        return on_col(where, where, h3_send.at[0], h3_recv.at[0], (1 - half) * Y + y)

    def some_g3(count):
        where = gram_ref.at[:, :count, :, top]
        return on_pair(where, where, g3_send.at[0], g3_recv.at[0], other_core)

    def some_h2(count):
        where = gram_ref.at[y, :count, :, bottom]
        return on_pair(where, where, h2_send.at[0], h2_recv.at[0], other_core)

    r_tiles = n_chip // 2

    @pl.when(early)
    def _():
        each(1, Y, lambda d: g2(wrap(y + d, Y)).start())
        some_h2(r_tiles).wait_recv()
        each(1, Y, lambda d: h3(wrap(y + d, Y)).start())
        all_g2().wait_recv()
        each(1, n_chip, lambda d: g3(wrap(chip + d, n_chip)).start())

    @pl.when(jnp.logical_not(early))
    def _():
        each(1, n_chip, lambda d: h2(wrap(chip + d, n_chip)).start())
        some_h2(r_tiles - 1).wait_recv()
        each(1, Y, lambda d: h3(wrap(y + d, Y)).start())

    def s3(t):
        return on_pair(sums_ref.at[chip, core], sums_ref.at[chip, core], s3_send.at[0], s3_recv.at[0], 2 * t + core)

    def all_s3():
        where = sums_ref.at[1:, core]
        return on_pair(where, where, s3_send.at[0], s3_recv.at[0], other_core)

    def s4():
        return on_pair(sums_ref.at[:, core], sums_ref.at[:, core], s4_send.at[0], s4_recv.at[0], other_core)

    def arrived_s4():
        where = sums_ref.at[:, 1 - core]
        return on_pair(where, where, s4_send.at[0], s4_recv.at[0], other_core)

    def g4(k, lanes):
        where = gram_ref.at[:, :, :, lanes]
        return on_pair(where, where, g4_send.at[k], g4_recv.at[k], other_core)

    all_s2().wait_recv()
    sums_ref[chip, core] = jnp.sum(sin[...].astype(jnp.float32), axis=0).astype(jnp.bfloat16)
    each(1, n_chip, lambda d: s3(wrap(chip + d, n_chip)).start())

    all_h3().wait_recv()
    g4(1, bottom).start()

    @pl.when(early)
    def _():
        some_g3(r_tiles - 1).wait_recv()

    @pl.when(jnp.logical_not(early))
    def _():
        some_g3(r_tiles).wait_recv()

    g4(0, top).start()
    all_s3().wait_recv()
    s4().start()
    g4(1, column(3 - core)).wait_recv()
    g4(0, column(1 - core)).wait_recv()
    arrived_s4().wait_recv()

    @pl.when(half == 0)
    def _():
        all_offers().wait_send()
        across().wait_send()

    all_blocks(0).wait_send()
    all_blocks(1).wait_send()
    all_deals().wait_send()
    all_gathers().wait_send()
    s1().wait_send()
    all_g1().wait_send()
    all_s2().wait_send()

    @pl.when(early)
    def _():
        all_g2().wait_send()
        each(1, n_chip, lambda d: g3(wrap(chip + d, n_chip)).wait_send())

    @pl.when(jnp.logical_not(early))
    def _():
        each(1, n_chip, lambda d: h2(wrap(chip + d, n_chip)).wait_send())

    g4(0, top).wait_send()
    g4(1, bottom).wait_send()
    all_h3().wait_send()
    all_s3().wait_send()
    s4().wait_send()


def exchange(owner, blocks, one_t, one_panel):
    n_pair, s_count, _, _, packed, orbitals = blocks.shape
    n_chip = n_pair // 2
    width = 2 * n_pair * packed
    rows = s_count * orbitals
    chunk = 2 * width // n_pair
    vmem = pl.BlockSpec(memory_space=pltpu.VMEM)
    f32, bf16 = jnp.float32, jnp.bfloat16
    sems = []
    for send, recv in ((2, 2), (1, 1), (1, 1), (1, 1), (1, 1), (1, 1), (1, 1), (n_chip, 1),
                       (n_chip, 1), (1, 1), (2, 2), (1, 1), (1, 1), (1, 1), (1, 1)):
        sems += [pltpu.SemaphoreType.DMA((send,)), pltpu.SemaphoreType.DMA((recv,))]
    return pl.pallas_call(
        exchange_kernel,
        out_shape=(
            jax.ShapeDtypeStruct((width, rows), bf16),
            jax.ShapeDtypeStruct((2, width, rows), bf16),
            jax.ShapeDtypeStruct((Y, width // Y // 8, 8, width), f32),
            jax.ShapeDtypeStruct((n_chip, 2, chunk, width), bf16),
        ),
        in_specs=[pl.BlockSpec(memory_space=pltpu.SMEM), vmem, vmem, vmem],
        out_specs=(vmem,) * 4,
        scratch_shapes=[
            pltpu.VMEM((n_pair, s_count, 2, 2, packed, orbitals), bf16),
            pltpu.VMEM((2 * BLOCK, 2 * BLOCK), bf16),
            pltpu.VMEM((Y, n_pair, packed, orbitals), bf16),
            pltpu.VMEM((n_pair, packed, orbitals), bf16),
            pltpu.VMEM((Y, n_pair, packed, orbitals), bf16),
            pltpu.VMEM((width // Y, width), f32),
            pltpu.VMEM((n_pair, 8, BLOCK), f32),
            pltpu.VMEM((n_chip, 2, chunk, width), bf16),
            pltpu.VMEM((n_chip, chunk, width), bf16),
            pltpu.VMEM((n_chip, chunk, width), bf16),
            pltpu.VMEM((n_chip, chunk, width), bf16),
            *sems,
        ],
        compiler_params=pltpu.CompilerParams(collective_id=0, has_side_effects=True, vmem_limit_bytes=32 << 20),
        name="regroup_exchange",
    )(owner, blocks, one_t, one_panel)


def per_device(two_rdm, one_rdm, panel_block):
    q_count, orbitals, r_count, _ = two_rdm.shape
    groups = lax.axis_size("pair")
    s_count = orbitals // groups
    panel_width = RPAN * orbitals
    col_index = lax.axis_index("col")
    first_orb = panel_block[0] * RPAN
    owner_col = first_orb // r_count
    within = first_orb % r_count
    turned = lax.dynamic_slice_in_dim(jnp.concatenate([two_rdm, two_rdm], 2), within, r_count, 2)
    blocks = jnp.transpose(turned, (3, 2, 0, 1)).reshape(groups, s_count, 2, 2, RPAN * q_count // 2, orbitals)
    one_cols = lax.dynamic_slice_in_dim(one_rdm, col_index * r_count, r_count, 1)
    one_t = lax.dynamic_slice_in_dim(jnp.concatenate([one_cols, one_cols], 1), within, r_count, 1).T
    one_panel = lax.dynamic_slice_in_dim(one_rdm, first_orb, RPAN, 1).T
    panel_t, tile_t, gram, sums_t = exchange(owner_col[None], blocks, one_t, one_panel)
    starts = col_index * r_count + jnp.arange(2, dtype=jnp.int32) * RPAN
    place = (jnp.arange(2, dtype=jnp.int32) + within // RPAN) % 2
    flags = jnp.concatenate([(starts >= first_orb + RPAN).astype(jnp.int32), place])
    sums_t = sums_t.reshape(2, panel_width, panel_width)
    triangle, updated = finish(
        flags, gram.reshape(panel_width, panel_width), sums_t, panel_t, tile_t, s_count, orbitals)
    return updated, triangle


def solution(mesh):
    return jax.shard_map(
        per_device,
        mesh=mesh,
        in_specs=(P("pair", None, "col", None), P(), P()),
        out_specs=(P("pair", None, "col", None), P()),
        check_vma=False,
    )
```

```python
import functools

import jax
import jax.numpy as jnp
from jax import lax
from jax.experimental import pallas as pl
from jax.experimental.pallas import tpu as pltpu
from jax.sharding import PartitionSpec as P

RPAN = 4
BLOCK = 128
STRIP = 8
EXACT = lax.Precision.HIGHEST
MESH = pl.DeviceIdType.MESH
Y = 8


def factor_block(work):
    for k in range(0, BLOCK, STRIP):
        tiles = (BLOCK - k) // STRIP
        left = work[k:BLOCK, 0:BLOCK]
        cols = [
            jnp.broadcast_to(left[:, k + j : k + j + 1], (BLOCK - k, BLOCK)).reshape(tiles, STRIP, BLOCK)
            for j in range(STRIP)
        ]
        rows_a = [jnp.broadcast_to(work[k + j : k + j + 1, :BLOCK], (STRIP, BLOCK)) for j in range(STRIP)]
        rows_b = [jnp.broadcast_to(work[k + j : k + j + 1, BLOCK:], (STRIP, BLOCK)) for j in range(STRIP)]
        entry = {
            (i, j): jnp.broadcast_to(cols[j][0, i : i + 1, :], (STRIP, BLOCK)) for j in range(STRIP) for i in range(j, STRIP)
        }
        for j in range(STRIP):
            inv = lax.rsqrt(entry[j, j])
            rows_a[j] = rows_a[j] * inv
            rows_b[j] = rows_b[j] * inv
            cols[j] = cols[j] * inv[None]
            low = {i: entry[i, j] * inv for i in range(j + 1, STRIP)}
            for i in range(j + 1, STRIP):
                for m in range(j + 1, i + 1):
                    entry[i, m] = entry[i, m] - low[i] * low[m]
                rows_a[i] = rows_a[i] - low[i] * rows_a[j]
                rows_b[i] = rows_b[i] - low[i] * rows_b[j]
                cols[i] = cols[i] - low[i][None] * cols[j]
        for j in range(STRIP):
            work[k + j : k + j + 1, :BLOCK] = rows_a[j][0:1]
            work[k + j : k + j + 1, BLOCK:] = rows_b[j][0:1]
        if tiles > 1:
            delta_a, delta_b = 0.0, 0.0
            for j in range(STRIP):
                delta_a = delta_a + cols[j][1:] * rows_a[j][None]
                delta_b = delta_b + cols[j][1:] * rows_b[j][None]
            below = BLOCK - k - STRIP
            work[k + STRIP : BLOCK, :BLOCK] = work[k + STRIP : BLOCK, :BLOCK] - delta_a.reshape(below, BLOCK)
            work[k + STRIP : BLOCK, BLOCK:] = work[k + STRIP : BLOCK, BLOCK:] - delta_b.reshape(below, BLOCK)


def factor_gram(scale, midway, gram_ref, tri_ref, high_ref, low_ref, left, right, work):
    n = left.shape[0]
    eye = (
        lax.broadcasted_iota(jnp.int32, (BLOCK, BLOCK), 0) == lax.broadcasted_iota(jnp.int32, (BLOCK, BLOCK), 1)
    ).astype(jnp.float32)
    lower = lax.broadcasted_iota(jnp.int32, (BLOCK, BLOCK), 0) >= lax.broadcasted_iota(jnp.int32, (BLOCK, BLOCK), 1)
    upper = lax.broadcasted_iota(jnp.int32, (BLOCK, BLOCK), 0) <= lax.broadcasted_iota(jnp.int32, (BLOCK, BLOCK), 1)

    def exact(a, b, contract):
        return lax.dot_general(a, b, (((contract,), (0,)), ((), ())), precision=EXACT, preferred_element_type=jnp.float32)

    left[...] = gram_ref[...].reshape(n, n)
    right[...] = jnp.zeros((n, n), jnp.float32)
    for o in range(0, n, BLOCK):
        end = o + BLOCK
        if o == n // 2:
            midway()
        here = work.at[o // BLOCK]
        here[:, :BLOCK] = left[o:end, o:end]
        here[:, BLOCK:] = eye
        factor_block(here)
        invert = jnp.where(lower, here[:, BLOCK:], 0.0)
        right[o:end, o:end] = invert
        if o:
            right[o:end, :o] = exact(invert, right[o:end, :o], 1)
            tri_ref[o:end, :o] = jnp.zeros((BLOCK, o), jnp.float32)
        tri_ref[o:end, o:end] = jnp.where(upper, here[:, :BLOCK], 0.0) / scale
        if end < n:
            left[o:end, end:] = exact(invert, left[o:end, end:], 1)
            tri_ref[o:end, end:] = left[o:end, end:] / scale
            for q in range(end, n, BLOCK):
                u = left[o:end, q:q + BLOCK]
                left[q:q + BLOCK, q:] = left[q:q + BLOCK, q:] - exact(u, left[o:end, q:], 0)
                right[q:q + BLOCK, :end] = right[q:q + BLOCK, :end] - exact(u, right[o:end, :end], 0)
    high = right[...].astype(jnp.bfloat16)
    high_ref[...] = high
    low_ref[...] = (right[...] - high.astype(jnp.float32)).astype(jnp.bfloat16)


def finish_kernel(flag_ref, high_ref, low_ref, sums_ref, panel_ref, tile_ref, out_ref, outer):
    def times(a, b, dims):
        return lax.dot_general(a, b, (dims, ((), ())), preferred_element_type=jnp.float32)

    high, low = high_ref[...], low_ref[...]
    basis = (times(high, panel_ref[...], ((1,), (0,))) + times(low, panel_ref[...], ((1,), (0,)))).astype(jnp.bfloat16)
    s_count, orbitals, r_count, _ = out_ref.shape
    per_half = r_count // 2
    for h in range(2):
        source = flag_ref[2 + h]
        sums = sums_ref[source]
        weights_t = (times(sums, high, ((1,), (1,))) + times(sums, low, ((1,), (1,)))).astype(jnp.bfloat16)
        product = times(weights_t, basis, ((1,), (0,)))
        outer[h] = tile_ref[source].astype(jnp.float32) - jnp.where(flag_ref[h] > 0, product, 0.0)
    for s in range(s_count):
        parts = [
            outer[h, r * BLOCK:(r + 1) * BLOCK, s * orbitals:(s + 1) * orbitals].T
            for h in range(2) for r in range(per_half)
        ]
        out_ref[s] = jnp.stack(parts, axis=1).astype(jnp.bfloat16)


def finish(flags, high, low, sums, panel_t, tile_t, s_count):
    n, rows = panel_t.shape
    whole = pl.BlockSpec(memory_space=pltpu.VMEM)
    return pl.pallas_call(
        finish_kernel,
        out_shape=jax.ShapeDtypeStruct((s_count, rows // s_count, 2 * n // BLOCK, BLOCK), jnp.bfloat16),
        in_specs=[pl.BlockSpec(memory_space=pltpu.SMEM)] + [whole] * 5,
        out_specs=whole,
        scratch_shapes=[pltpu.VMEM((2, n, rows), jnp.float32)],
        compiler_params=pltpu.CompilerParams(vmem_limit_bytes=24 << 20),
        cost_estimate=pl.CostEstimate(flops=12 * n**3, bytes_accessed=10 * n * n, transcendentals=0),
        name="apply",
    )(flags, high, low, sums, panel_t, tile_t)


def wrap(value, count):
    return jnp.where(value >= count, value - count, value)


def each(start, stop, body):
    lax.fori_loop(start, stop, lambda k, c: (body(k), c)[1], 0)


def exchange_kernel(scale, owner_ref, x_ref, one_ref, one_panel_ref, panel_ref, gt_ref, sums_ref, tri_ref, high_ref,
                    low_ref, gram_ref, left, right, work, land, order, picks, chosen, raw, gpart, gin, spart, score, shalf, sin,
                    a_send, a_recv, p_send, p_recv, q_send, q_recv, m_send, m_recv, c_send, c_recv,
                    g1_send, g1_recv, g2_send, g2_recv,
                    g3_send, g3_recv, h2_send, h2_recv, h3_send, h3_recv, g4_send, g4_recv,
                    s1_send, s1_recv, s2_send, s2_recv, s3_send, s3_recv, s4_send, s4_recv):
    pair = lax.axis_index("pair")
    colm = lax.axis_index("col")
    n_pair = lax.axis_size("pair")
    n_chip = n_pair // 2
    chip, core = pair // 2, lax.rem(pair, 2)
    half, y = colm // Y, lax.rem(colm, Y)
    other_core = 2 * chip + 1 - core
    width = panel_ref.shape[0]
    part = width // Y
    wide = width // BLOCK
    s_count = x_ref.shape[1]
    over_last = (((1,), (1,)), ((), ()))

    def on_pair(src, dst, send, recv, k):
        return pltpu.make_async_remote_copy(
            src_ref=src, dst_ref=dst, send_sem=send, recv_sem=recv, device_id={"pair": k}, device_id_type=MESH)

    def on_col(src, dst, send, recv, k):
        return pltpu.make_async_remote_copy(
            src_ref=src, dst_ref=dst, send_sem=send, recv_sem=recv, device_id={"col": k}, device_id_type=MESH)

    barrier = pltpu.get_barrier_semaphore()
    each(1, n_pair, lambda d: pl.semaphore_signal(
        barrier, inc=1, device_id={"pair": wrap(pair + d, n_pair)}, device_id_type=MESH))
    each(1, Y, lambda d: pl.semaphore_signal(
        barrier, inc=1, device_id={"col": half * Y + wrap(y + d, Y)}, device_id_type=MESH))
    pl.semaphore_signal(barrier, inc=1, device_id={"col": (1 - half) * Y + y}, device_id_type=MESH)
    pl.semaphore_wait(barrier, n_pair + Y - 1)

    def offer(k):
        return on_col(x_ref.at[:, k // 2, 0, lax.rem(k, 2)], picks.at[y], p_send.at[0], p_recv.at[0], k)

    def all_offers():
        return on_col(picks.at[1:], picks.at[1:], p_send.at[0], p_recv.at[0], (1 - half) * Y + y)

    @pl.when(half == 0)
    def _():
        each(1, Y, lambda d: offer(wrap(y + d, Y)).start())

    def block(h, peer):
        return on_pair(x_ref.at[peer, :, h], land.at[pair, :, h], a_send.at[h], a_recv.at[h], peer)

    def all_blocks(h):
        return on_pair(x_ref.at[1:, :, h], land.at[1:, :, h], a_send.at[h], a_recv.at[h], other_core)

    each(1, n_pair, lambda d: block(0, wrap(pair + d, n_pair)).start())
    land[pair] = x_ref[pair]

    size = 2 * BLOCK
    row = lax.broadcasted_iota(jnp.int32, (size, size), 0)
    col = lax.broadcasted_iota(jnp.int32, (size, size), 1)
    q, r = row & (BLOCK - 1), row // BLOCK
    order[...] = (col == (q // 4) * 8 + r * 4 + (q & 3)).astype(jnp.float32).astype(jnp.bfloat16)
    q_row = lax.broadcasted_iota(jnp.int32, (BLOCK, BLOCK), 0)

    def columns_of(moved, ones, u, s):
        placed = jnp.dot(order[...], moved.reshape(size, BLOCK), preferred_element_type=jnp.float32)
        out = []
        for v in range(2):
            diagonal = jnp.where(q_row == pair * s_count + s, ones[2 * u + v:2 * u + v + 1, :], 0.0)
            out.append(diagonal - placed[v * BLOCK:(v + 1) * BLOCK])
        return jnp.concatenate(out, axis=0).astype(jnp.bfloat16)

    def build(h):
        ones = one_ref[h * wide:(h + 1) * wide, :]
        for s in range(s_count):
            for u in range(2):
                gt_ref[h, u * size:(u + 1) * size, s * BLOCK:(s + 1) * BLOCK] = columns_of(land[:, s, h, u], ones, u, s)

    def across():
        return on_col(chosen, chosen, q_send.at[0], q_recv.at[0], (1 - half) * Y + y)

    def deal(peer):
        return on_pair(chosen.at[peer], raw.at[y, pair], m_send.at[0], m_recv.at[0], peer)

    def all_deals():
        return on_pair(raw.at[y, 1:], raw.at[y, 1:], m_send.at[0], m_recv.at[0], other_core)

    def gather(k):
        return on_col(raw.at[y], raw.at[y], c_send.at[0], c_recv.at[0], half * Y + k)

    def all_gathers():
        return on_col(raw.at[1:], raw.at[1:], c_send.at[0], c_recv.at[0], (1 - half) * Y + y)

    @pl.when(half == 0)
    def _():
        picks[y] = x_ref[:, y // 2, 0, lax.rem(y, 2)]
        all_offers().wait_recv()
        chosen[...] = picks[owner_ref[0]]
        across().start()

    @pl.when(half == 1)
    def _():
        across().wait_recv()

    each(1, n_pair, lambda d: deal(wrap(pair + d, n_pair)).start())
    raw[y, pair] = chosen[pair]
    each(1, n_pair, lambda d: block(1, wrap(pair + d, n_pair)).start())
    all_deals().wait_recv()
    each(1, Y, lambda d: gather(wrap(y + d, Y)).start())
    for h in range(2):
        all_blocks(h).wait_recv()
        build(h)
    all_gathers().wait_recv()
    for k in range(Y):
        s, u = k // 2, k % 2
        panel_ref[u * size:(u + 1) * size, s * BLOCK:(s + 1) * BLOCK] = columns_of(raw[k], one_panel_ref[...], u, s)

    chunk = sums_ref.shape[2]
    rows_at_once = 2 * BLOCK
    count = rows_at_once // (2 * chunk)
    for h in range(2):
        for k in range(width // rows_at_once):
            out = lax.dot_general(gt_ref[h, k * rows_at_once:(k + 1) * rows_at_once, :], panel_ref[...], over_last,
                                  preferred_element_type=jnp.float32).astype(jnp.bfloat16)
            at = (h * (width // rows_at_once) + k) * count
            spart[at:at + count] = out.reshape(count, 2, chunk, width)

    def s1():
        return on_pair(spart.at[:, 1 - core], score, s1_send.at[0], s1_recv.at[0], other_core)

    s1().start()

    gpart[...] = lax.dot_general(panel_ref[pl.ds(pl.multiple_of(y * part, part), part), :], panel_ref[...], over_last,
                                 preferred_element_type=jnp.float32)

    def column(c):
        return pl.ds(pl.multiple_of(c * BLOCK, BLOCK), BLOCK)

    def g1(i, slot):
        src = gpart.at[pl.ds(pl.multiple_of((i // wide) * 8, 8), 8), column(lax.rem(i, wide))]
        return on_pair(src, gin.at[slot], g1_send.at[0], g1_recv.at[0], i)

    each(1, n_pair, lambda d: g1(wrap(pair + d, n_pair), pair).start())
    my_r, my_c = pair // wide, lax.rem(pair, wide)
    gin[pair] = gpart[pl.ds(pl.multiple_of(my_r * 8, 8), 8), column(my_c)]

    s1().wait_recv()

    def add_cores(k):
        shalf[k] = (spart[k, core].astype(jnp.float32) + score[k].astype(jnp.float32)).astype(jnp.bfloat16)

    each(0, n_chip, add_cores)

    def s2(t, slot):
        return on_pair(shalf.at[t], sin.at[slot], s2_send.at[0], s2_recv.at[0], 2 * t + core)

    each(1, n_chip, lambda d: s2(wrap(chip + d, n_chip), chip).start())
    sin[chip] = shalf[chip]

    def all_g1():
        return on_pair(gin.at[1:], gin.at[1:], g1_send.at[0], g1_recv.at[0], other_core)

    def all_s2():
        return on_pair(shalf.at[1:], sin.at[1:], s2_send.at[0], s2_recv.at[0], other_core)

    all_g1().wait_recv()
    gram_ref[y, my_r, :, column(my_c)] = jnp.sum(gin[...], axis=0)

    early = lax.rem(chip, 2) == 0
    top, bottom = column(core), column(2 + core)
    mine = gram_ref.at[y, my_r, :, column(my_c)]
    tall = gram_ref.at[:, my_r, :, top]
    flat = gram_ref.at[y, :, :, bottom]

    def g2(k):
        return on_col(mine, mine, g2_send.at[0], g2_recv.at[0], half * Y + k)

    def all_g2():
        where = gram_ref.at[1:, my_r, :, top]
        return on_col(where, where, g2_send.at[0], g2_recv.at[0], (1 - half) * Y + y)

    def g3(t):
        return on_pair(tall, tall, g3_send.at[t], g3_recv.at[0], 2 * t + core)

    def h2(t):
        return on_pair(mine, mine, h2_send.at[t], h2_recv.at[0], 2 * t + core)

    def h3(k):
        return on_col(flat, flat, h3_send.at[0], h3_recv.at[0], half * Y + k)

    def all_h3():
        where = gram_ref.at[1:, :, :, bottom]
        return on_col(where, where, h3_send.at[0], h3_recv.at[0], (1 - half) * Y + y)

    def some_g3(count):
        where = gram_ref.at[:, :count, :, top]
        return on_pair(where, where, g3_send.at[0], g3_recv.at[0], other_core)

    def some_h2(count):
        where = gram_ref.at[y, :count, :, bottom]
        return on_pair(where, where, h2_send.at[0], h2_recv.at[0], other_core)

    r_tiles = n_chip // 2

    @pl.when(early)
    def _():
        each(1, Y, lambda d: g2(wrap(y + d, Y)).start())
        some_h2(r_tiles).wait_recv()
        each(1, Y, lambda d: h3(wrap(y + d, Y)).start())
        all_g2().wait_recv()
        each(1, n_chip, lambda d: g3(wrap(chip + d, n_chip)).start())

    @pl.when(jnp.logical_not(early))
    def _():
        each(1, n_chip, lambda d: h2(wrap(chip + d, n_chip)).start())
        some_h2(r_tiles - 1).wait_recv()
        each(1, Y, lambda d: h3(wrap(y + d, Y)).start())

    def s3(t):
        return on_pair(sums_ref.at[chip, core], sums_ref.at[chip, core], s3_send.at[0], s3_recv.at[0], 2 * t + core)

    def all_s3():
        where = sums_ref.at[1:, core]
        return on_pair(where, where, s3_send.at[0], s3_recv.at[0], other_core)

    def s4():
        return on_pair(sums_ref.at[:, core], sums_ref.at[:, core], s4_send.at[0], s4_recv.at[0], other_core)

    def arrived_s4():
        where = sums_ref.at[:, 1 - core]
        return on_pair(where, where, s4_send.at[0], s4_recv.at[0], other_core)

    def g4(k, lanes):
        where = gram_ref.at[:, :, :, lanes]
        return on_pair(where, where, g4_send.at[k], g4_recv.at[k], other_core)

    all_s2().wait_recv()
    sums_ref[chip, core] = jnp.sum(sin[...].astype(jnp.float32), axis=0).astype(jnp.bfloat16)
    each(1, n_chip, lambda d: s3(wrap(chip + d, n_chip)).start())

    all_h3().wait_recv()
    g4(1, bottom).start()

    @pl.when(early)
    def _():
        some_g3(r_tiles - 1).wait_recv()

    @pl.when(jnp.logical_not(early))
    def _():
        some_g3(r_tiles).wait_recv()

    g4(0, top).start()
    g4(1, column(3 - core)).wait_recv()
    g4(0, column(1 - core)).wait_recv()

    def midway():
        all_s3().wait_recv()
        s4().start()

    factor_gram(scale, midway, gram_ref, tri_ref, high_ref, low_ref, left, right, work)
    arrived_s4().wait_recv()

    @pl.when(half == 0)
    def _():
        all_offers().wait_send()
        across().wait_send()

    all_blocks(0).wait_send()
    all_blocks(1).wait_send()
    all_deals().wait_send()
    all_gathers().wait_send()
    s1().wait_send()
    all_g1().wait_send()
    all_s2().wait_send()

    @pl.when(early)
    def _():
        all_g2().wait_send()
        each(1, n_chip, lambda d: g3(wrap(chip + d, n_chip)).wait_send())

    @pl.when(jnp.logical_not(early))
    def _():
        each(1, n_chip, lambda d: h2(wrap(chip + d, n_chip)).wait_send())

    g4(0, top).wait_send()
    g4(1, bottom).wait_send()
    all_h3().wait_send()
    all_s3().wait_send()
    s4().wait_send()


def exchange(owner, blocks, one_t, one_panel, scale):
    n_pair, s_count, _, _, packed, orbitals = blocks.shape
    n_chip = n_pair // 2
    width = 2 * n_pair * packed
    rows = s_count * orbitals
    chunk = 2 * width // n_pair
    vmem = pl.BlockSpec(memory_space=pltpu.VMEM)
    f32, bf16 = jnp.float32, jnp.bfloat16
    sems = []
    for send, recv in ((2, 2), (1, 1), (1, 1), (1, 1), (1, 1), (1, 1), (1, 1), (n_chip, 1),
                       (n_chip, 1), (1, 1), (2, 2), (1, 1), (1, 1), (1, 1), (1, 1)):
        sems += [pltpu.SemaphoreType.DMA((send,)), pltpu.SemaphoreType.DMA((recv,))]
    return pl.pallas_call(
        functools.partial(exchange_kernel, scale),
        out_shape=(
            jax.ShapeDtypeStruct((width, rows), bf16),
            jax.ShapeDtypeStruct((2, width, rows), bf16),
            jax.ShapeDtypeStruct((n_chip, 2, chunk, width), bf16),
            jax.ShapeDtypeStruct((width, width), f32),
            jax.ShapeDtypeStruct((width, width), bf16),
            jax.ShapeDtypeStruct((width, width), bf16),
        ),
        in_specs=[pl.BlockSpec(memory_space=pltpu.SMEM), vmem, vmem, vmem],
        out_specs=(vmem,) * 6,
        scratch_shapes=[
            pltpu.VMEM((Y, width // Y // 8, 8, width), f32),
            pltpu.VMEM((width, width), f32),
            pltpu.VMEM((width, width), f32),
            pltpu.VMEM((width // BLOCK, BLOCK, 2 * BLOCK), f32),
            pltpu.VMEM((n_pair, s_count, 2, 2, packed, orbitals), bf16),
            pltpu.VMEM((2 * BLOCK, 2 * BLOCK), bf16),
            pltpu.VMEM((Y, n_pair, packed, orbitals), bf16),
            pltpu.VMEM((n_pair, packed, orbitals), bf16),
            pltpu.VMEM((Y, n_pair, packed, orbitals), bf16),
            pltpu.VMEM((width // Y, width), f32),
            pltpu.VMEM((n_pair, 8, BLOCK), f32),
            pltpu.VMEM((n_chip, 2, chunk, width), bf16),
            pltpu.VMEM((n_chip, chunk, width), bf16),
            pltpu.VMEM((n_chip, chunk, width), bf16),
            pltpu.VMEM((n_chip, chunk, width), bf16),
            *sems,
        ],
        compiler_params=pltpu.CompilerParams(collective_id=0, has_side_effects=True, vmem_limit_bytes=32 << 20),
        name="regroup_exchange",
    )(owner, blocks, one_t, one_panel)


def per_device(two_rdm, one_rdm, panel_block):
    q_count, orbitals, r_count, _ = two_rdm.shape
    groups = lax.axis_size("pair")
    s_count = orbitals // groups
    panel_width = RPAN * orbitals
    col_index = lax.axis_index("col")
    first_orb = panel_block[0] * RPAN
    owner_col = first_orb // r_count
    within = first_orb % r_count
    turned = lax.dynamic_slice_in_dim(jnp.concatenate([two_rdm, two_rdm], 2), within, r_count, 2)
    blocks = jnp.transpose(turned, (3, 2, 0, 1)).reshape(groups, s_count, 2, 2, RPAN * q_count // 2, orbitals)
    one_cols = lax.dynamic_slice_in_dim(one_rdm, col_index * r_count, r_count, 1)
    one_t = lax.dynamic_slice_in_dim(jnp.concatenate([one_cols, one_cols], 1), within, r_count, 1).T
    one_panel = lax.dynamic_slice_in_dim(one_rdm, first_orb, RPAN, 1).T
    panel_t, tile_t, sums_t, triangle, high, low = exchange(owner_col[None], blocks, one_t, one_panel, orbitals)
    starts = col_index * r_count + jnp.arange(2, dtype=jnp.int32) * RPAN
    place = (jnp.arange(2, dtype=jnp.int32) + within // RPAN) % 2
    flags = jnp.concatenate([(starts >= first_orb + RPAN).astype(jnp.int32), place])
    sums_t = sums_t.reshape(2, panel_width, panel_width)
    return finish(flags, high, low, sums_t, panel_t, tile_t, s_count), triangle


def solution(mesh):
    return jax.shard_map(
        per_device,
        mesh=mesh,
        in_specs=(P("pair", None, "col", None), P(), P()),
        out_specs=(P("pair", None, "col", None), P()),
        check_vma=False,
    )
```
